512 devices in a mesh: dom: 32 (over z, x), feat: 16 (over y, core).
Axes of the slice: x: 4, y: 8, z: 8, core: 2. Of those that a mesh axis runs over, the one named last changes fastest.
Arguments:
- features: bfloat16 [768, 65536], P('feat', 'dom'), may hold values from -6 to 6
- neighbors: int32 [16, 65536], P(None, 'dom'), may hold values from 0 to 3071
- degree: int32 [65536], P('dom'), may hold values from 1 to 16
- send_rows: int32 [32, 32, 32], P('dom'), may hold values from 0 to 2047
- labels: int32 [65536], P('dom'), may hold values from 0 to 1
- w_self: bfloat16 [768, 512], replicated, may hold values from -0.21875 to 0.21875
- w_neigh: bfloat16 [768, 512], replicated, may hold values from -0.21875 to 0.21875
- bias: float32 [512], replicated, may hold values from -3 to 3
- a_self: float32 [512], replicated, may hold values from -0.5 to 0.5
- a_neigh: float32 [512], replicated, may hold values from -0.5 to 0.5
Outputs:
- logits: float32 [65536], P('dom')
- grad_self: float32 [768, 512], P('feat')
- grad_neigh: float32 [768, 512], P('feat')
The draws below stay inside these ranges and needn't reach their ends.
Inputs may be any that keep to these rules, and one draw needn't show every extreme that they name: `neighbors`: slots under 2048 are the partition's own nodes, the others nodes sent by other partitions.
All inputs are finite; a program needn't handle non-finite values.
Results may differ from the reference program's by a relative error of at most 0.012.
The reference program's roundings to bfloat16 on the way (of `aggregated` and `dpre`) count: a program that leaves them out, or rounds other values in their place, can miss the bound.
Values may be sent and summed in bfloat16 or wider, within the bound.
No kernel may reach another device: no remote copies, remote signals or barrier semaphores. Data moves between devices by JAX's collectives and lax.ppermute only.
A program may use at most 64 MiB of HBM per device.

```python
import jax
import jax.numpy as jnp
from jax import lax

D_IN = 768
HID = 512
FAN = 16
NP = 2048
B = 32
NODES = 65536
N_DOM = 32


def place_ends(array, rng, least, high):
    longest = array.shape.index(max(array.shape))
    spots = []
    for shift in (0, 1):
        where = [jax.random.randint(jax.random.fold_in(rng, axis), (), 0, length) for axis, length in enumerate(array.shape)]
        where[longest] = (where[longest] + shift) % array.shape[longest]
        spots.append(tuple(where))
    return array.at[spots[0]].set(least).at[spots[1]].set(high)


def levels(stream_key, shape, shards, low, largest):
    def one(axis_at, parts):
        draws = jax.random.uniform(jax.random.fold_in(jax.random.fold_in(stream_key, 6), axis_at), (parts,), jnp.float32, low / len(shards), largest / len(shards))
        return jnp.repeat(jnp.exp(draws), shape[axis_at] // parts).reshape((-1,) + (1,) * (len(shape) - axis_at - 1))

    loudness = one(*shards[0])
    for cut in shards[1:]:
        loudness = loudness * one(*cut)
    return loudness


def noise(own_key, shape, spread, reach, shards=(), kind=jnp.bfloat16):
    values = spread * jax.random.normal(own_key, shape, jnp.float32)
    if shards:
        values = values * levels(own_key, shape, shards, -0.22, 0.18)
    return jnp.clip(values, -reach, reach).astype(kind)


def setup_inputs(seed: int = 0) -> dict:
    arg_keys = jax.random.split(jax.random.key(seed), 11)
    features = noise(arg_keys[0], (D_IN, NODES), 1.0, 6.0, ((0, 16), (1, 32)))
    neighbors = place_ends(jax.random.randint(arg_keys[1], (FAN, NODES), 0, NP + N_DOM * B), jax.random.fold_in(arg_keys[1], 1), 0, (NP + N_DOM * B) - 1).astype(jnp.int32)
    degree = place_ends(jax.random.randint(arg_keys[2], (NODES,), 1, FAN + 1), jax.random.fold_in(arg_keys[2], 1), 1, FAN).astype(jnp.int32)
    send_rows = place_ends(jax.random.randint(arg_keys[3], (N_DOM, N_DOM, B), 0, NP), jax.random.fold_in(arg_keys[3], 1), 0, NP - 1).astype(jnp.int32)
    labels = place_ends(jax.random.randint(arg_keys[4], (NODES,), 0, 2), jax.random.fold_in(arg_keys[4], 1), 0, 1).astype(jnp.int32)
    w_self = noise(arg_keys[5], (D_IN, HID), D_IN ** -0.5, 0.21875)
    w_neigh = noise(arg_keys[6], (D_IN, HID), D_IN ** -0.5, 0.21875)
    bias = noise(arg_keys[7], (HID,), 0.5, 3.0, (), jnp.float32)
    a_self = noise(arg_keys[8], (HID,), (HID // 4) ** -0.5, 0.5, (), jnp.float32)
    a_neigh = noise(arg_keys[9], (HID,), (HID // 4) ** -0.5, 0.5, (), jnp.float32)
    return {"features": features, "neighbors": neighbors, "degree": degree, "send_rows": send_rows, "labels": labels, "w_self": w_self, "w_neigh": w_neigh, "bias": bias, "a_self": a_self, "a_neigh": a_neigh}


def reference(features, neighbors, degree, send_rows, labels, w_self, w_neigh, bias, a_self, a_neigh):
    partitions = N_DOM

    def table_index(part_index):
        own_nodes = part_index * NP + jnp.arange(NP, dtype=jnp.int32)
        remote_nodes = jnp.arange(partitions, dtype=jnp.int32)[:, None] * NP + send_rows[:, part_index, :]
        return jnp.concatenate([own_nodes, remote_nodes.reshape(-1)]).astype(jnp.int32)

    table_global = lax.map(table_index, jnp.arange(partitions, dtype=jnp.int32))
    local_lists = neighbors.reshape(FAN, partitions, NP).transpose(1, 0, 2)
    global_lists = jax.vmap(lambda table_row, listed: table_row[listed])(table_global, local_lists)
    global_flat = global_lists.transpose(1, 0, 2).reshape(FAN, NP * partitions)
    neighbor_mask = jnp.arange(FAN)[:, None] < degree[None, :]
    inverse = 1.0 / degree.astype(jnp.float32)
    mask_parts = neighbor_mask.reshape(FAN, partitions, NP).transpose(1, 0, 2)

    def aggregate(packed):
        listed, masked, scales = packed
        summed = jnp.zeros((D_IN, NP), jnp.float32)
        for neighbor_slot in range(FAN):
            taken = features[:, listed[neighbor_slot]].astype(jnp.float32)
            summed = summed + jnp.where(masked[neighbor_slot][None, :], taken, 0.0)
        return (summed * scales[None, :]).astype(jnp.bfloat16)

    aggregated = lax.map(aggregate, (global_lists, mask_parts, inverse.reshape(partitions, NP)))
    aggregated = aggregated.transpose(1, 0, 2).reshape(D_IN, NP * partitions)
    dims = (((0,), (0,)), ((), ()))
    preact = lax.dot_general(features, w_self, dims, preferred_element_type=jnp.float32) + lax.dot_general(aggregated, w_neigh, dims, preferred_element_type=jnp.float32) + bias
    hidden = jnp.maximum(preact, 0.0)
    score_self = jnp.sum(hidden * a_self, axis=1)
    score_neigh = jnp.sum(hidden * a_neigh, axis=1)
    logits = score_self + jnp.sum(jnp.where(neighbor_mask, score_neigh[global_flat], 0.0), axis=0) * inverse
    loss_scale = float(NP * N_DOM) ** -0.5
    dlogit = (jax.nn.sigmoid(logits) - labels.astype(jnp.float32)) * loss_scale
    weighted = jnp.where(neighbor_mask, (dlogit * inverse)[None, :], 0.0)
    dneigh = jnp.zeros((NP * N_DOM,), jnp.float32).at[global_flat].add(weighted)
    dpre = jnp.where(preact > 0, dlogit[:, None] * a_self + dneigh[:, None] * a_neigh, 0.0).astype(jnp.bfloat16)
    grad_self = jnp.dot(features, dpre, preferred_element_type=jnp.float32)
    grad_neigh = jnp.dot(aggregated, dpre, preferred_element_type=jnp.float32)
    return (logits, grad_self, grad_neigh)
```

```python
import jax
import jax.numpy as jnp
from jax import lax
from jax.experimental import pallas as pl
from jax.experimental.pallas import tpu as pltpu
from jax.sharding import PartitionSpec as P

F32 = jnp.float32
BF16 = jnp.bfloat16
I32 = jnp.int32

SL = 48
NP = 2048
NB = 16
PARTS = 32
SENT = 1024
SLOTS = 3072
FAN = 16
HID = 512
FIELD = 512


def call(kernel, out_shape, name, **kw):
    return pl.pallas_call(kernel, out_shape=out_shape, name=name, **kw)


def sds(shape, dtype):
    return jax.ShapeDtypeStruct(shape, dtype)


def split3(x):
    hi = x.astype(BF16)
    rest = x - hi.astype(F32)
    mid = rest.astype(BF16)
    low = (rest - mid.astype(F32)).astype(BF16)
    return hi, mid, low


def send_kernel(feat_ref, send_ref, out_ref):
    feats = feat_ref[...]
    columns = jnp.transpose(send_ref[...], (1, 0))
    lanes = lax.broadcasted_iota(I32, (128, NP), 1)
    out_ref[...] = jnp.zeros_like(out_ref)
    for r in range(SENT // 128):
        onehot = jnp.where(columns[:, r : r + 1] == lanes, 1.0, 0.0).astype(BF16)
        rows = lax.dot_general(onehot, feats, (((1,), (1,)), ((), ())), preferred_element_type=F32)
        out_ref[pl.ds(r * 128, 128), 0:SL] = rows.astype(BF16)


def count_kernel(nbr_ref, deg_ref, feat_ref, cnt_ref, own_ref):
    width = nbr_ref.shape[1]
    rows8 = lax.broadcasted_iota(I32, (8, 128), 0)
    for lane_block in range(width // 128):
        lanes = pl.ds(lane_block * 128, 128)
        idx = nbr_ref[:, lanes]
        valid = lax.broadcasted_iota(I32, (FAN, 128), 0) < deg_ref[:, lanes]
        field = lax.shift_right_logical(idx, 9)
        q = jnp.where(valid, jnp.bitwise_and(idx, FIELD - 1), -1)
        v = jnp.left_shift(jnp.ones_like(idx), field * 5)
        qs = [jnp.broadcast_to(q[k : k + 1], (8, 128)) for k in range(FAN)]
        vs = [jnp.broadcast_to(v[k : k + 1], (8, 128)) for k in range(FAN)]

        def row(r, carry, qs=qs, vs=vs, lanes=lanes):
            base = pl.multiple_of(r * 16, 16)
            packed = []
            for half in range(2):
                t = rows8 + (base + 8 * half)
                acc = jnp.zeros((8, 128), I32)
                for k in range(FAN):
                    acc = acc + jnp.where(qs[k] == t, vs[k], 0)
                packed.append(acc)
            both = jnp.concatenate(packed, axis=0)
            for j in range(SLOTS // FIELD):
                count = jnp.bitwise_and(lax.shift_right_logical(both, 5 * j), 31)
                cnt_ref[pl.ds(j * FIELD + base, 16), lanes] = count.astype(F32).astype(BF16)
            return carry

        lax.fori_loop(0, FIELD // 16, row, 0)
    own_ref[...] = jnp.dot(feat_ref[...], cnt_ref[0:NP, :], preferred_element_type=F32)


def finish_kernel(recv_ref, cnt_ref, own_ref, deg_ref, feat_ref, out_ref):
    width = own_ref.shape[1]
    far = lax.dot_general(recv_ref[...], cnt_ref[...], (((0,), (0,)), ((), ())), preferred_element_type=F32)
    inverse = 1.0 / deg_ref[...].astype(F32)
    agg = ((own_ref[...] + far[0:SL, :]) * inverse).astype(BF16)
    feats = feat_ref[...]
    for b in range(width // 128):
        out_ref[b, 0:SL, :] = feats[:, b * 128 : (b + 1) * 128]
        out_ref[b, SL : 2 * SL, :] = agg[:, b * 128 : (b + 1) * 128]


def preact_kernel(block_ref, w_ref, par_ref, mask_ref, score_ref):
    block = block_ref[...].reshape(2 * SL * NB, 128)
    pre = lax.dot_general(block, w_ref[...], (((0,), (0,)), ((), ())), preferred_element_type=F32)
    pre = jnp.transpose(pre, (1, 0)) + par_ref[:, 0:1]
    hidden = jnp.maximum(pre, 0.0)
    mask_ref[...] = jnp.where(pre > 0, 1.0, 0.0).astype(BF16)
    own = jnp.sum(hidden * par_ref[:, 1:2], axis=0, keepdims=True)
    neigh = jnp.sum(hidden * par_ref[:, 2:3], axis=0, keepdims=True)
    both = jnp.concatenate([own, neigh, jnp.zeros((6, 128), F32)], axis=0)
    for b in range(NB):
        score_ref[b] = both


def lane_gather(row, idx):
    return jnp.take_along_axis(jnp.broadcast_to(row, idx.shape), idx, axis=1)


def boundary_score_kernel(score_ref, send_ref, out_ref):
    idx = send_ref[...]
    low = jnp.bitwise_and(idx, 127)
    high = lax.shift_right_logical(idx, 7)
    acc = jnp.zeros((PARTS, 128), F32)
    for b in range(NB):
        acc = jnp.where(high == b, lane_gather(score_ref[b, 1:2, :], low), acc)
    for p in range(PARTS):
        out_ref[p] = acc[p : p + 1, :]


def dense_rows(ref):
    lane = lax.broadcasted_iota(I32, (8, 128), 1)
    acc = jnp.zeros((8, 128), F32)
    for g in range(4):
        rows = jnp.concatenate([ref[4 * r + g] for r in range(8)], axis=0)
        rows = pltpu.roll(rows, 32 * g, 1) if g else rows
        acc = jnp.where(lax.shift_right_logical(lane, 5) == g, rows, acc)
    return acc


def logit_kernel(score_ref, far_ref, nbr_ref, deg_ref, label_ref, cnt_ref, logit_ref, dlogit_ref, slot_ref, out_ref, table, weight):
    step = pl.program_id(0)
    width = cnt_ref.shape[1]

    @pl.when(step == 0)
    def _():
        for b in range(NB):
            table[b : b + 1, :] = score_ref[b, 1:2, :]
        table[NB:, :] = dense_rows(far_ref)

        def one(f, carry):
            lanes = pl.ds(pl.multiple_of(f * 128, 128), 128)
            idx = nbr_ref[:, lanes]
            low = jnp.bitwise_and(idx, 127)
            high = lax.shift_right_logical(idx, 7)
            acc = jnp.zeros((FAN, 128), F32)
            for r in range(SLOTS // 128):
                acc = jnp.where(high == r, lane_gather(table[r : r + 1, :], low), acc)
            degree = deg_ref[:, lanes]
            valid = lax.broadcasted_iota(I32, (FAN, 128), 0) < degree
            inverse = 1.0 / degree.astype(F32)
            total = jnp.sum(jnp.where(valid, acc, 0.0), axis=0, keepdims=True)
            logits = score_ref[f, 0:1, :] + total * inverse
            logit_ref[:, lanes] = logits
            dlogit = (jax.nn.sigmoid(logits) - label_ref[:, lanes].astype(F32)) * (float(NP * PARTS) ** -0.5)
            dlogit_ref[:, lanes] = dlogit
            hi, mid, low_part = split3(dlogit * inverse)
            rows = jnp.concatenate([hi.astype(F32), mid.astype(F32), low_part.astype(F32), jnp.zeros((13, 128), F32)], axis=0)
            weight[:, lanes] = rows.astype(BF16)
            return carry

        lax.fori_loop(0, NB, one, 0)
        slot_ref[...] = jnp.zeros_like(slot_ref)

    part = lax.dot_general(
        weight[:, pl.ds(pl.multiple_of(step * width, 128), width)],
        cnt_ref[...],
        (((1,), (1,)), ((), ())),
        preferred_element_type=F32,
    )
    slot_ref[...] += part[0:1, :] + part[1:2, :] + part[2:3, :]

    @pl.when(step == pl.num_programs(0) - 1)
    def _():
        for r in range(8):
            row = slot_ref[:, pl.ds(NP + r * 128, 128)]
            for g in range(4):
                out_ref[4 * r + g] = pltpu.roll(row, 128 - 32 * g, 1) if g else row


def grad_kernel(ret_ref, send_ref, slot_ref, dlogit_ref, par_ref, mask_ref, block_ref, out_ref, dneigh, acc):
    step = pl.program_id(0)
    per = mask_ref.shape[0]

    @pl.when(step == 0)
    def _():
        send = jnp.transpose(send_ref[...], (1, 0))
        back = jnp.transpose(dense_rows(ret_ref), (1, 0))
        lane = lax.broadcasted_iota(I32, (128, 128), 1)
        for f in range(NB):
            total = jnp.zeros((128, 128), F32)
            for r in range(8):
                total = total + jnp.where(send[:, r : r + 1] == lane + f * 128, back[:, r : r + 1], 0.0)
            lanes = slice(f * 128, (f + 1) * 128)
            dneigh[:, lanes] = slot_ref[:, lanes] + jnp.sum(total, axis=0, keepdims=True)
        acc[...] = jnp.zeros_like(acc)

    for b in range(per):
        lanes = pl.ds(pl.multiple_of((step * per + b) * 128, 128), 128)
        grad = par_ref[:, 1:2] * dlogit_ref[:, lanes] + par_ref[:, 2:3] * dneigh[:, lanes]
        dpre = jnp.where(mask_ref[b].astype(F32) > 0, grad, 0.0).astype(BF16)
        acc[...] += lax.dot_general(block_ref[b], dpre, (((1,), (1,)), ((), ())), preferred_element_type=F32)

    @pl.when(step == pl.num_programs(0) - 1)
    def _():
        for tile in range(12):
            for half in range(2):
                for c in range(4):
                    row = tile * 8 + half * 4
                    out_ref[(tile * 2 + half) * 4 + c] = acc[row : row + 4, c * 128 : (c + 1) * 128]


def sum_kernel(in_ref, out_ref):
    for c in range(3):
        total = in_ref[c]
        for p in range(1, PARTS):
            total = total + in_ref[3 * p + c]
        for p in range(PARTS):
            out_ref[3 * p + c] = total


def place_kernel(in_ref, self_ref, neigh_ref):
    for tile in range(12):
        for half in range(2):
            for c in range(4):
                value = in_ref[(tile * 2 + half) * 4 + c]
                row = (tile % 6) * 8 + half * 4
                ref = self_ref if tile < 6 else neigh_ref
                ref[row : row + 4, c * 128 : (c + 1) * 128] = value


def whole(shape):
    return pl.BlockSpec(shape, lambda *_: (0,) * len(shape))


def body(features, neighbors, degree, send_rows, labels, w_self, w_neigh, bias, a_self, a_neigh):
    degree = degree.reshape(1, NP)
    labels = labels.reshape(1, NP)
    send_dense = send_rows.reshape(8, 128)
    send_wide = jnp.pad(send_rows[0], ((0, 0), (0, 96)))
    params = jnp.pad(jnp.stack([bias, a_self, a_neigh], axis=1), ((0, 0), (0, 125)))
    weights = jnp.stack([w_self.reshape(NB, SL, HID), w_neigh.reshape(NB, SL, HID)], axis=1).reshape(NB * 2 * SL, HID)

    outgoing = call(send_kernel, sds((SENT, 128), BF16), "send")(features, send_dense)
    incoming = lax.all_to_all(outgoing, "dom", split_axis=0, concat_axis=0, tiled=True)

    wide = 256
    counts, own = call(
        count_kernel,
        (sds((SLOTS, NP), BF16), sds((SL, NP), F32)),
        "count",
        grid=(NP // wide,),
        in_specs=[
            pl.BlockSpec((FAN, wide), lambda i: (0, i)),
            pl.BlockSpec((1, wide), lambda i: (0, i)),
            whole((SL, NP)),
        ],
        out_specs=(pl.BlockSpec((SLOTS, wide), lambda i: (0, i)), pl.BlockSpec((SL, wide), lambda i: (0, i))),
    )(neighbors, degree, features)

    wide = 512
    block = call(
        finish_kernel,
        sds((NB, 2 * SL, 128), BF16),
        "finish",
        grid=(NP // wide,),
        in_specs=[
            whole((SENT, 128)),
            pl.BlockSpec((SENT, wide), lambda i: (2, i)),
            pl.BlockSpec((SL, wide), lambda i: (0, i)),
            pl.BlockSpec((1, wide), lambda i: (0, i)),
            pl.BlockSpec((SL, wide), lambda i: (0, i)),
        ],
        out_specs=pl.BlockSpec((wide // 128, 2 * SL, 128), lambda i: (i, 0, 0)),
    )(incoming, counts, own, degree, features)
    mine = lax.all_to_all(block, "feat", split_axis=0, concat_axis=0, tiled=True)

    mask, scores = call(preact_kernel, (sds((HID, 128), BF16), sds((NB, 8, 128), F32)), "preact")(mine, weights, params)
    scores = lax.all_to_all(scores, "feat", split_axis=0, concat_axis=0, tiled=True)

    score_out = call(boundary_score_kernel, sds((PARTS, 1, 128), F32), "bscore")(scores, send_wide)
    score_in = lax.all_to_all(score_out, "dom", split_axis=0, concat_axis=0, tiled=True)
    masks = jnp.broadcast_to(mask[None], (NB, HID, 128))
    masks, _ = lax.optimization_barrier((masks, score_out))
    masks = lax.all_to_all(masks, "feat", split_axis=0, concat_axis=0, tiled=True)

    wide = 512
    logits, dlogit, slot, slot_out = call(
        logit_kernel,
        (sds((1, NP), F32), sds((1, NP), F32), sds((1, SLOTS), F32), sds((PARTS, 1, 128), F32)),
        "logit",
        grid=(NP // wide,),
        in_specs=[
            whole((NB, 8, 128)),
            whole((PARTS, 1, 128)),
            whole((FAN, NP)),
            whole((1, NP)),
            whole((1, NP)),
            pl.BlockSpec((SLOTS, wide), lambda i: (0, i)),
        ],
        out_specs=(whole((1, NP)), whole((1, NP)), whole((1, SLOTS)), whole((PARTS, 1, 128))),
        scratch_shapes=[pltpu.VMEM((SLOTS // 128, 128), F32), pltpu.VMEM((16, NP), BF16)],
    )(scores, score_in, neighbors, degree, labels, counts)
    returned = lax.all_to_all(slot_out, "dom", split_axis=0, concat_axis=0, tiled=True)

    per = 4
    partial = call(
        grad_kernel,
        sds((96, 4, 128), F32),
        "grad",
        grid=(NB // per,),
        in_specs=[
            whole((PARTS, 1, 128)),
            whole((8, 128)),
            whole((1, SLOTS)),
            whole((1, NP)),
            whole((HID, 128)),
            pl.BlockSpec((per, HID, 128), lambda i: (i, 0, 0)),
            pl.BlockSpec((per, 2 * SL, 128), lambda i: (i, 0, 0)),
        ],
        out_specs=whole((96, 4, 128)),
        scratch_shapes=[pltpu.VMEM((1, NP), F32), pltpu.VMEM((2 * SL, HID), F32)],
    )(returned, send_dense, slot, dlogit, params, masks, block)
    shares = lax.all_to_all(partial, "dom", split_axis=0, concat_axis=0, tiled=True)
    summed = call(sum_kernel, sds((96, 4, 128), F32), "sum")(shares)
    summed = lax.all_to_all(summed, "dom", split_axis=0, concat_axis=0, tiled=True)
    grad_self, grad_neigh = call(place_kernel, (sds((SL, HID), F32), sds((SL, HID), F32)), "place")(summed)
    return (logits.reshape(NP), grad_self, grad_neigh)


def solution(mesh):
    return jax.shard_map(
        body,
        mesh=mesh,
        in_specs=(
            P("feat", "dom"),
            P(None, "dom"),
            P("dom"),
            P("dom", None, None),
            P("dom"),
            P(),
            P(),
            P(),
            P(),
            P(),
        ),
        out_specs=(P("dom"), P("feat", None), P("feat", None)),
        check_vma=False,
    )
```

```python
import jax
import jax.numpy as jnp
from jax import lax
from jax.experimental import pallas as pl
from jax.experimental.pallas import tpu as pltpu
from jax.sharding import PartitionSpec as P

F32 = jnp.float32
BF16 = jnp.bfloat16
I32 = jnp.int32

SL = 48
NP = 2048
NB = 16
PARTS = 32
B = 32
SENT = 1024
SLOTS = 3072
FAN = 16
HID = 512
UNROLL = 2
FIELD = 512


def call(kernel, out_shape, name, **kw):
    return pl.pallas_call(kernel, out_shape=out_shape, name=name, **kw)


def sds(shape, dtype):
    return jax.ShapeDtypeStruct(shape, dtype)


def split3(x):
    hi = x.astype(BF16)
    rest = x - hi.astype(F32)
    mid = rest.astype(BF16)
    low = (rest - mid.astype(F32)).astype(BF16)
    return hi, mid, low


def send_kernel(feat_ref, send_ref, out_ref):
    feats = feat_ref[...]
    columns = jnp.transpose(send_ref[0], (1, 0))
    lanes = lax.broadcasted_iota(I32, (B, NP), 1)
    out_ref[...] = jnp.zeros_like(out_ref)
    for r in range(PARTS // 4):
        onehot = jnp.concatenate(
            [jnp.where(columns[:, p : p + 1] == lanes, 1.0, 0.0).astype(BF16) for p in range(4 * r, 4 * r + 4)], axis=0
        )
        rows = lax.dot_general(onehot, feats, (((1,), (1,)), ((), ())), preferred_element_type=F32)
        out_ref[pl.ds(r * 128, 128), 0:SL] = rows.astype(BF16)


def count_kernel(nbr_ref, deg_ref, feat_ref, cnt_ref, own_ref):
    width = nbr_ref.shape[1]
    rows8 = lax.broadcasted_iota(I32, (8, 128), 0)
    for lane_block in range(width // 128):
        lanes = pl.ds(lane_block * 128, 128)
        idx = nbr_ref[:, lanes]
        valid = lax.broadcasted_iota(I32, (FAN, 128), 0) < deg_ref[:, lanes]
        field = lax.shift_right_logical(idx, 9)
        q = jnp.where(valid, jnp.bitwise_and(idx, FIELD - 1), -1)
        v = jnp.left_shift(jnp.ones_like(idx), field * 5)
        qs = [jnp.broadcast_to(q[k : k + 1], (8, 128)) for k in range(FAN)]
        vs = [jnp.broadcast_to(v[k : k + 1], (8, 128)) for k in range(FAN)]

        def row(r, carry, qs=qs, vs=vs, lanes=lanes):
            for u in range(UNROLL):
                base = pl.multiple_of(r * (16 * UNROLL), 16 * UNROLL) + 16 * u
                packed = []
                for half in range(2):
                    t = rows8 + (base + 8 * half)
                    acc = jnp.zeros((8, 128), I32)
                    for k in range(FAN):
                        acc = acc + jnp.where(qs[k] == t, vs[k], 0)
                    packed.append(acc)
                both = jnp.concatenate(packed, axis=0)
                for j in range(SLOTS // FIELD):
                    count = jnp.bitwise_and(lax.shift_right_logical(both, 5 * j), 31)
                    rows = pl.ds(pl.multiple_of(j * FIELD + base, 16), 16)
                    cnt_ref[rows, lanes] = count.astype(F32).astype(BF16)
            return carry

        lax.fori_loop(0, FIELD // (16 * UNROLL), row, 0)
    own_ref[...] = jnp.dot(feat_ref[...], cnt_ref[0:NP, :], preferred_element_type=F32)


def finish_kernel(recv_ref, cnt_ref, own_ref, deg_ref, feat_ref, out_ref):
    width = own_ref.shape[1]
    far = lax.dot_general(recv_ref[...], cnt_ref[...], (((0,), (0,)), ((), ())), preferred_element_type=F32)
    inverse = 1.0 / deg_ref[...].astype(F32)
    agg = ((own_ref[...] + far[0:SL, :]) * inverse).astype(BF16)
    feats = feat_ref[...]
    for b in range(width // 128):
        out_ref[b, 0:SL, :] = feats[:, b * 128 : (b + 1) * 128]
        out_ref[b, SL : 2 * SL, :] = agg[:, b * 128 : (b + 1) * 128]


def preact_kernel(block_ref, w_ref, par_ref, mask_ref, score_ref):
    block = block_ref[...].reshape(2 * SL * NB, 128)
    pre = lax.dot_general(block, w_ref[...], (((0,), (0,)), ((), ())), preferred_element_type=F32)
    pre = jnp.transpose(pre, (1, 0)) + par_ref[:, 0:1]
    hidden = jnp.maximum(pre, 0.0)
    mask_ref[...] = jnp.where(pre > 0, 1.0, 0.0).astype(BF16)
    own = jnp.sum(hidden * par_ref[:, 1:2], axis=0, keepdims=True)
    neigh = jnp.sum(hidden * par_ref[:, 2:3], axis=0, keepdims=True)
    both = jnp.concatenate([own, neigh, jnp.zeros((6, 128), F32)], axis=0)
    for b in range(NB):
        score_ref[b] = both


def lane_gather(row, idx):
    return jnp.take_along_axis(jnp.broadcast_to(row, idx.shape), idx, axis=1)


def boundary_score_kernel(score_ref, send_ref, out_ref):
    idx = jnp.concatenate([send_ref[0], jnp.zeros((PARTS, 96), I32)], axis=1)
    low = jnp.bitwise_and(idx, 127)
    high = lax.shift_right_logical(idx, 7)
    acc = jnp.zeros((PARTS, 128), F32)
    for b in range(NB):
        acc = jnp.where(high == b, lane_gather(score_ref[b, 1:2, :], low), acc)
    for p in range(PARTS):
        out_ref[p] = acc[p : p + 1, :]


def own_logit_kernel(score_ref, nbr_ref, deg_ref, out_ref):
    def one(f, carry):
        lanes = pl.ds(pl.multiple_of(f * 128, 128), 128)
        idx = nbr_ref[:, lanes]
        low = jnp.bitwise_and(idx, 127)
        high = lax.shift_right_logical(idx, 7)
        acc = jnp.zeros((FAN, 128), F32)
        for r in range(NB):
            acc = jnp.where(high == r, lane_gather(score_ref[r, 1:2, :], low), acc)
        valid = lax.broadcasted_iota(I32, (FAN, 128), 0) < deg_ref[:, lanes]
        out_ref[:, lanes] = jnp.sum(jnp.where(valid, acc, 0.0), axis=0, keepdims=True)
        return carry

    lax.fori_loop(0, NB, one, 0)


def dense_rows(ref):
    lane = lax.broadcasted_iota(I32, (8, 128), 1)
    acc = jnp.zeros((8, 128), F32)
    for g in range(4):
        rows = jnp.concatenate([ref[4 * r + g] for r in range(8)], axis=0)
        rows = pltpu.roll(rows, 32 * g, 1) if g else rows
        acc = jnp.where(lax.shift_right_logical(lane, 5) == g, rows, acc)
    return acc


def logit_kernel(score_ref, own_ref, far_ref, nbr_ref, deg_ref, label_ref, cnt_ref, logit_ref, dlogit_ref, slot_ref, out_ref, table, weight):
    step = pl.program_id(0)
    width = cnt_ref.shape[1]

    @pl.when(step == 0)
    def _():
        table[...] = dense_rows(far_ref)

        def one(f, carry):
            lanes = pl.ds(pl.multiple_of(f * 128, 128), 128)
            idx = nbr_ref[:, lanes]
            low = jnp.bitwise_and(idx, 127)
            high = lax.shift_right_logical(idx, 7)
            acc = jnp.zeros((FAN, 128), F32)
            for r in range(SENT // 128):
                acc = jnp.where(high == NB + r, lane_gather(table[r : r + 1, :], low), acc)
            degree = deg_ref[:, lanes]
            valid = lax.broadcasted_iota(I32, (FAN, 128), 0) < degree
            inverse = 1.0 / degree.astype(F32)
            total = own_ref[:, lanes] + jnp.sum(jnp.where(valid, acc, 0.0), axis=0, keepdims=True)
            logits = score_ref[f, 0:1, :] + total * inverse
            logit_ref[:, lanes] = logits
            dlogit = (jax.nn.sigmoid(logits) - label_ref[:, lanes].astype(F32)) * (float(NP * PARTS) ** -0.5)
            dlogit_ref[:, lanes] = dlogit
            hi, mid, low_part = split3(dlogit * inverse)
            rows = jnp.concatenate([hi.astype(F32), mid.astype(F32), low_part.astype(F32), jnp.zeros((13, 128), F32)], axis=0)
            weight[:, lanes] = rows.astype(BF16)
            return carry

        lax.fori_loop(0, NB, one, 0)
        slot_ref[...] = jnp.zeros_like(slot_ref)

    part = lax.dot_general(
        weight[:, pl.ds(pl.multiple_of(step * width, 128), width)],
        cnt_ref[...],
        (((1,), (1,)), ((), ())),
        preferred_element_type=F32,
    )
    slot_ref[...] += part[0:1, :] + part[1:2, :] + part[2:3, :]

    @pl.when(step == pl.num_programs(0) - 1)
    def _():
        for r in range(8):
            row = slot_ref[:, pl.ds(NP + r * 128, 128)]
            for g in range(4):
                out_ref[4 * r + g] = pltpu.roll(row, 128 - 32 * g, 1) if g else row


def grad_kernel(ret_ref, send_ref, slot_ref, dlogit_ref, par_ref, mask_ref, block_ref, out_ref, dneigh, acc):
    step = pl.program_id(0)
    per = mask_ref.shape[0]

    @pl.when(step == 0)
    def _():
        send = jnp.transpose(send_ref[0], (1, 0))
        back = jnp.transpose(jnp.concatenate([ret_ref[p] for p in range(PARTS)], axis=0), (1, 0))[0:B]
        lane = lax.broadcasted_iota(I32, (B, 128), 1)

        def one(f, carry):
            total = jnp.zeros((B, 128), F32)
            for p in range(PARTS):
                total = total + jnp.where(send[:, p : p + 1] == lane + f * 128, back[:, p : p + 1], 0.0)
            lanes = pl.ds(pl.multiple_of(f * 128, 128), 128)
            dneigh[:, lanes] = slot_ref[:, lanes] + jnp.sum(total, axis=0, keepdims=True)
            return carry

        lax.fori_loop(0, NB, one, 0)
        acc[...] = jnp.zeros_like(acc)

    for b in range(per):
        lanes = pl.ds(pl.multiple_of((step * per + b) * 128, 128), 128)
        grad = par_ref[:, 1:2] * dlogit_ref[:, lanes] + par_ref[:, 2:3] * dneigh[:, lanes]
        dpre = jnp.where(mask_ref[b].astype(F32) > 0, grad, 0.0).astype(BF16)
        acc[...] += lax.dot_general(block_ref[b], dpre, (((1,), (1,)), ((), ())), preferred_element_type=F32)

    @pl.when(step == pl.num_programs(0) - 1)
    def _():
        for tile in range(12):
            for half in range(2):
                for c in range(4):
                    row = tile * 8 + half * 4
                    out_ref[(tile * 2 + half) * 4 + c] = acc[row : row + 4, c * 128 : (c + 1) * 128]


def sum_kernel(in_ref, out_ref):
    for c in range(3):
        total = in_ref[c]
        for p in range(1, PARTS):
            total = total + in_ref[3 * p + c]
        for p in range(PARTS):
            out_ref[3 * p + c] = total


def place_kernel(in_ref, self_ref, neigh_ref):
    for tile in range(12):
        for half in range(2):
            for c in range(4):
                value = in_ref[(tile * 2 + half) * 4 + c]
                row = (tile % 6) * 8 + half * 4
                ref = self_ref if tile < 6 else neigh_ref
                ref[row : row + 4, c * 128 : (c + 1) * 128] = value


def whole(shape):
    return pl.BlockSpec(shape, lambda *_: (0,) * len(shape))


def resident():
    return pl.BlockSpec(memory_space=pltpu.VMEM)


def exchange(x, axis):
    x = lax.all_to_all(x, axis, split_axis=0, concat_axis=0, tiled=True)
    return pltpu.with_memory_space_constraint(x, pltpu.VMEM)


def body(features, neighbors, degree, send_rows, labels, w_self, w_neigh, bias, a_self, a_neigh):
    degree = degree.reshape(1, NP)
    labels = labels.reshape(1, NP)
    params = jnp.pad(jnp.stack([bias, a_self, a_neigh], axis=1), ((0, 0), (0, 125)))
    weights = jnp.stack([w_self.reshape(NB, SL, HID), w_neigh.reshape(NB, SL, HID)], axis=1).reshape(NB * 2 * SL, HID)

    outgoing = call(send_kernel, sds((SENT, 128), BF16), "send")(features, send_rows)
    incoming = exchange(outgoing, "dom")

    wide = 256
    counts, own = call(
        count_kernel,
        (sds((SLOTS, NP), BF16), sds((SL, NP), F32)),
        "count",
        grid=(NP // wide,),
        in_specs=[
            pl.BlockSpec((FAN, wide), lambda i: (0, i)),
            pl.BlockSpec((1, wide), lambda i: (0, i)),
            whole((SL, NP)),
        ],
        out_specs=(pl.BlockSpec((SLOTS, wide), lambda i: (0, i)), pl.BlockSpec((SL, wide), lambda i: (0, i))),
    )(neighbors, degree, features)

    wide = 512
    block = call(
        finish_kernel,
        sds((NB, 2 * SL, 128), BF16),
        "finish",
        grid=(NP // wide,),
        in_specs=[
            resident(),
            pl.BlockSpec((SENT, wide), lambda i: (2, i)),
            pl.BlockSpec((SL, wide), lambda i: (0, i)),
            pl.BlockSpec((1, wide), lambda i: (0, i)),
            pl.BlockSpec((SL, wide), lambda i: (0, i)),
        ],
        out_specs=pl.BlockSpec((wide // 128, 2 * SL, 128), lambda i: (i, 0, 0)),
    )(incoming, counts, own, degree, features)
    mine = exchange(block, "feat")

    mask, scores = call(preact_kernel, (sds((HID, 128), BF16), sds((NB, 8, 128), F32)), "preact")(mine, weights, params)
    scores = exchange(scores, "feat")

    mask, scores = lax.optimization_barrier((mask, scores))
    masks = lax.all_gather(mask, "feat", axis=0, tiled=False)
    score_out = call(boundary_score_kernel, sds((PARTS, 1, 128), F32), "bscore")(scores, send_rows)
    score_in = exchange(score_out, "dom")
    own_total = call(own_logit_kernel, sds((1, NP), F32), "ownlogit")(scores, neighbors, degree)

    wide = 512
    logits, dlogit, slot, slot_out = call(
        logit_kernel,
        (sds((1, NP), F32), sds((1, NP), F32), sds((1, SLOTS), F32), sds((PARTS, 1, 128), F32)),
        "logit",
        grid=(NP // wide,),
        in_specs=[
            resident(),
            whole((1, NP)),
            resident(),
            whole((FAN, NP)),
            whole((1, NP)),
            whole((1, NP)),
            pl.BlockSpec((SLOTS, wide), lambda i: (0, i)),
        ],
        out_specs=(whole((1, NP)), whole((1, NP)), whole((1, SLOTS)), whole((PARTS, 1, 128))),
        scratch_shapes=[pltpu.VMEM((SENT // 128, 128), F32), pltpu.VMEM((16, NP), BF16)],
    )(scores, own_total, score_in, neighbors, degree, labels, counts)
    returned = exchange(slot_out, "dom")

    per = 4
    partial = call(
        grad_kernel,
        sds((96, 4, 128), F32),
        "grad",
        grid=(NB // per,),
        in_specs=[
            resident(),
            whole((1, B, PARTS)),
            whole((1, SLOTS)),
            whole((1, NP)),
            whole((HID, 128)),
            pl.BlockSpec((per, HID, 128), lambda i: (i, 0, 0)),
            pl.BlockSpec((per, 2 * SL, 128), lambda i: (i, 0, 0)),
        ],
        out_specs=whole((96, 4, 128)),
        scratch_shapes=[pltpu.VMEM((1, NP), F32), pltpu.VMEM((2 * SL, HID), F32)],
    )(returned, send_rows, slot, dlogit, params, masks, block)
    shares = exchange(partial, "dom")
    summed = call(sum_kernel, sds((96, 4, 128), F32), "sum")(shares)
    summed = exchange(summed, "dom")
    grad_self, grad_neigh = call(place_kernel, (sds((SL, HID), F32), sds((SL, HID), F32)), "place")(summed)
    return (logits.reshape(NP), grad_self, grad_neigh)


def solution(mesh):
    return jax.shard_map(
        body,
        mesh=mesh,
        in_specs=(
            P("feat", "dom"),
            P(None, "dom"),
            P("dom"),
            P("dom", None, None),
            P("dom"),
            P(),
            P(),
            P(),
            P(),
            P(),
        ),
        out_specs=(P("dom"), P("feat", None), P("feat", None)),
        check_vma=False,
    )
```

```python
import jax
import jax.numpy as jnp
from jax import lax
from jax.experimental import pallas as pl
from jax.experimental.pallas import tpu as pltpu
from jax.sharding import PartitionSpec as P

F32 = jnp.float32
BF16 = jnp.bfloat16
I32 = jnp.int32

SL = 48
NP = 2048
NB = 16
PARTS = 32
B = 32
SENT = 1024
SLOTS = 3072
FAN = 16
HID = 512
UNROLL = 11
WIDE = 256
OWN_FIELD = 352
FAR_FIELD = 176


def call(kernel, out_shape, name, **kw):
    return pl.pallas_call(kernel, out_shape=out_shape, name=name, **kw)


def sds(shape, dtype):
    return jax.ShapeDtypeStruct(shape, dtype)


def split3(x):
    hi = x.astype(BF16)
    rest = x - hi.astype(F32)
    mid = rest.astype(BF16)
    low = (rest - mid.astype(F32)).astype(BF16)
    return hi, mid, low


def send_kernel(feat_ref, send_ref, out_ref):
    feats = feat_ref[...]
    columns = jnp.transpose(send_ref[0], (1, 0))
    lanes = lax.broadcasted_iota(I32, (B, NP), 1)
    out_ref[...] = jnp.zeros_like(out_ref)
    for r in range(PARTS // 4):
        onehot = jnp.concatenate(
            [jnp.where(columns[:, p : p + 1] == lanes, 1.0, 0.0).astype(BF16) for p in range(4 * r, 4 * r + 4)], axis=0
        )
        rows = lax.dot_general(onehot, feats, (((1,), (1,)), ((), ())), preferred_element_type=F32)
        out_ref[pl.ds(r * 128, 128), 0:SL] = rows.astype(BF16)


def build_counts(nbr_ref, deg_ref, cnt_ref, first, size, field):
    rows8 = lax.broadcasted_iota(I32, (8, 128), 0)

    def block(lane_block, carry):
        lanes = pl.ds(pl.multiple_of(lane_block * 128, 128), 128)
        idx = nbr_ref[:, lanes] - first
        valid = (lax.broadcasted_iota(I32, (FAN, 128), 0) < deg_ref[:, lanes]) & (idx >= 0) & (idx < size)
        which = jnp.zeros_like(idx)
        for j in range(1, 6):
            which = which + jnp.where(idx >= j * field, 1, 0)
        q = jnp.where(valid, idx - which * field, -1)
        v = jnp.left_shift(jnp.ones_like(idx), which * 5)
        qs = [jnp.broadcast_to(q[k : k + 1], (8, 128)) for k in range(FAN)]
        vs = [jnp.broadcast_to(v[k : k + 1], (8, 128)) for k in range(FAN)]

        def row(r, inner):
            for u in range(UNROLL):
                base = pl.multiple_of(r * (16 * UNROLL), 16 * UNROLL) + 16 * u
                packed = []
                for part in range(2):
                    t = rows8 + (base + 8 * part)
                    acc = jnp.zeros((8, 128), I32)
                    for k in range(FAN):
                        acc = acc + jnp.where(qs[k] == t, vs[k], 0)
                    packed.append(acc)
                both = jnp.concatenate(packed, axis=0)
                for j in range(6):
                    count = jnp.bitwise_and(lax.shift_right_logical(both, 5 * j), 31)
                    rows = pl.ds(pl.multiple_of(j * field + base, 16), 16)
                    cnt_ref[rows, lanes] = count.astype(F32).astype(BF16)
            return inner

        return lax.fori_loop(0, field // (16 * UNROLL), row, carry)

    lax.fori_loop(0, WIDE // 128, block, 0)


def own_kernel(nbr_ref, deg_ref, feat_ref, own_ref, cnt):
    build_counts(nbr_ref, deg_ref, cnt, 0, NP, OWN_FIELD)
    own_ref[...] = jnp.dot(feat_ref[...], cnt[0:NP, :], preferred_element_type=F32)


def finish_kernel(recv_ref, nbr_ref, deg_ref, own_ref, feat_ref, out_ref, cnt, recv):
    @pl.when(pl.program_id(0) == 0)
    def _():
        recv[...] = jnp.transpose(recv_ref[...].astype(F32), (1, 0))[0:SL].astype(BF16)

    build_counts(nbr_ref, deg_ref, cnt, NP, SENT, FAR_FIELD)
    far = jnp.dot(recv[...], cnt[0:SENT, :], preferred_element_type=F32)
    inverse = 1.0 / deg_ref[...].astype(F32)
    agg = ((own_ref[...] + far) * inverse).astype(BF16)
    feats = feat_ref[...]
    for b in range(WIDE // 128):
        out_ref[b, 0:SL, :] = feats[:, b * 128 : (b + 1) * 128]
        out_ref[b, SL : 2 * SL, :] = agg[:, b * 128 : (b + 1) * 128]


def columns(*refs):
    rows = [ref[...] for ref in refs] + [jnp.zeros((8 - len(refs), HID), F32)]
    return jnp.transpose(jnp.concatenate(rows, axis=0), (1, 0))


def preact_kernel(block_ref, ws_ref, wn_ref, bias_ref, as_ref, an_ref, mask_ref, score_ref):
    dims = (((0,), (0,)), ((), ()))
    pre = lax.dot_general(block_ref[:, 0:SL, :].reshape(SL * NB, 128), ws_ref[...], dims, preferred_element_type=F32)
    pre = pre + lax.dot_general(block_ref[:, SL : 2 * SL, :].reshape(SL * NB, 128), wn_ref[...], dims, preferred_element_type=F32)
    par = columns(bias_ref, as_ref, an_ref)
    pre = jnp.transpose(pre, (1, 0)) + par[:, 0:1]
    hidden = jnp.maximum(pre, 0.0)
    mask_ref[...] = jnp.where(pre > 0, 1.0, 0.0).astype(BF16)
    own = jnp.sum(hidden * par[:, 1:2], axis=0, keepdims=True)
    neigh = jnp.sum(hidden * par[:, 2:3], axis=0, keepdims=True)
    both = jnp.concatenate([own, neigh, jnp.zeros((6, 128), F32)], axis=0)
    for b in range(NB):
        score_ref[b] = both


def lane_gather(row, idx):
    return jnp.take_along_axis(jnp.broadcast_to(row, idx.shape), idx, axis=1)


def boundary_score_kernel(score_ref, send_ref, out_ref):
    idx = jnp.concatenate([send_ref[0], jnp.zeros((PARTS, 96), I32)], axis=1)
    low = jnp.bitwise_and(idx, 127)
    high = lax.shift_right_logical(idx, 7)
    acc = jnp.zeros((PARTS, 128), F32)
    for b in range(NB):
        acc = jnp.where(high == b, lane_gather(score_ref[b, 1:2, :], low), acc)
    for p in range(PARTS):
        out_ref[p] = acc[p : p + 1, :]


def own_logit_kernel(score_ref, nbr_ref, deg_ref, out_ref):
    def one(f, carry):
        lanes = pl.ds(pl.multiple_of(f * 128, 128), 128)
        idx = nbr_ref[:, lanes]
        low = jnp.bitwise_and(idx, 127)
        high = lax.shift_right_logical(idx, 7)
        acc = jnp.zeros((FAN, 128), F32)
        for r in range(NB):
            acc = jnp.where(high == r, lane_gather(score_ref[r, 1:2, :], low), acc)
        valid = lax.broadcasted_iota(I32, (FAN, 128), 0) < deg_ref[:, lanes]
        out_ref[:, lanes] = jnp.sum(jnp.where(valid, acc, 0.0), axis=0, keepdims=True)
        return carry

    lax.fori_loop(0, NB, one, 0)


def dense_rows(ref):
    lane = lax.broadcasted_iota(I32, (8, 128), 1)
    acc = jnp.zeros((8, 128), F32)
    for g in range(4):
        rows = jnp.concatenate([ref[4 * r + g] for r in range(8)], axis=0)
        rows = pltpu.roll(rows, 32 * g, 1) if g else rows
        acc = jnp.where(lax.shift_right_logical(lane, 5) == g, rows, acc)
    return acc


def logit_kernel(score_ref, own_ref, far_ref, nbr_ref, deg_ref, label_ref, logit_ref, dlogit_ref, slot_ref, out_ref, table, acc_ref):
    table[...] = dense_rows(far_ref)
    acc_ref[...] = jnp.zeros_like(acc_ref)
    highs = SLOTS // 128
    high_rows = lax.broadcasted_iota(I32, (highs, 128), 0)
    low_rows = lax.broadcasted_iota(I32, (128, 128), 0)

    def one(f, carry):
        lanes = pl.ds(pl.multiple_of(f * 128, 128), 128)
        idx = nbr_ref[:, lanes]
        low = jnp.bitwise_and(idx, 127)
        high = lax.shift_right_logical(idx, 7)
        acc = jnp.zeros((FAN, 128), F32)
        for r in range(SENT // 128):
            acc = jnp.where(high == NB + r, lane_gather(table[r : r + 1, :], low), acc)
        degree = deg_ref[:, lanes]
        valid = lax.broadcasted_iota(I32, (FAN, 128), 0) < degree
        inverse = 1.0 / degree.astype(F32)
        total = own_ref[:, lanes] + jnp.sum(jnp.where(valid, acc, 0.0), axis=0, keepdims=True)
        logits = score_ref[f, 0:1, :] + total * inverse
        logit_ref[:, lanes] = logits
        dlogit = (jax.nn.sigmoid(logits) - label_ref[:, lanes].astype(F32)) * (float(NP * PARTS) ** -0.5)
        dlogit_ref[:, lanes] = dlogit
        thirds = [t.astype(F32) for t in split3(dlogit * inverse)]
        high = jnp.where(valid, high, -1)
        for k in range(0, FAN, 2):
            left, right = [], []
            for kk in (k, k + 1):
                hit = high[kk : kk + 1] == high_rows
                left.append(jnp.concatenate([jnp.where(hit, t, 0.0) for t in thirds], axis=0).astype(BF16))
                right.append(jnp.where(low[kk : kk + 1] == low_rows, 1.0, 0.0).astype(BF16))
            acc_ref[...] += lax.dot_general(
                jnp.concatenate(left, axis=1),
                jnp.concatenate(right, axis=1),
                (((1,), (1,)), ((), ())),
                preferred_element_type=F32,
            )
        return carry

    lax.fori_loop(0, NB, one, 0)
    slot = acc_ref[0:highs] + acc_ref[highs : 2 * highs] + acc_ref[2 * highs : 3 * highs]
    slot_ref[...] = slot
    for r in range(8):
        row = slot[NB + r : NB + r + 1, :]
        for g in range(4):
            out_ref[4 * r + g] = pltpu.roll(row, 128 - 32 * g, 1) if g else row


def grad_kernel(ret_ref, send_ref, slot_ref, dlogit_ref, as_ref, an_ref, mask_ref, block_ref, out_ref, dneigh, wide_s, wide_n, acc):
    step = pl.program_id(0)
    per = mask_ref.shape[0]

    @pl.when(step == 0)
    def _():
        send = jnp.transpose(send_ref[0], (1, 0))
        back = jnp.transpose(jnp.concatenate([ret_ref[p] for p in range(PARTS)], axis=0), (1, 0))[0:B]
        lane = lax.broadcasted_iota(I32, (8, 128), 1)
        totals = [jnp.zeros((8, 128), F32) for _ in range(NB)]
        for p in range(PARTS):
            for c in range(B // 8):
                node = jnp.broadcast_to(send[8 * c : 8 * c + 8, p : p + 1], (8, 128)) - lane
                value = jnp.broadcast_to(back[8 * c : 8 * c + 8, p : p + 1], (8, 128))
                for f in range(NB):
                    totals[f] = totals[f] + jnp.where(node == f * 128, value, 0.0)
        for f in range(NB):
            lanes = slice(f * 128, (f + 1) * 128)
            dneigh[:, lanes] = slot_ref[f : f + 1, :] + jnp.sum(totals[f], axis=0, keepdims=True)
        par = columns(as_ref, an_ref)
        wide_s[...] = jnp.broadcast_to(par[:, 0:1], (HID, 128))
        wide_n[...] = jnp.broadcast_to(par[:, 1:2], (HID, 128))
        acc[...] = jnp.zeros_like(acc)

    for b in range(per):
        lanes = pl.ds(pl.multiple_of((step * per + b) * 128, 128), 128)
        grad = wide_s[...] * dlogit_ref[:, lanes] + wide_n[...] * dneigh[:, lanes]
        dpre = grad.astype(BF16) * mask_ref[b]
        acc[...] += lax.dot_general(block_ref[b], dpre, (((1,), (1,)), ((), ())), preferred_element_type=F32)

    @pl.when(step == pl.num_programs(0) - 1)
    def _():
        for tile in range(12):
            for half in range(2):
                for c in range(4):
                    row = tile * 8 + half * 4
                    out_ref[(tile * 2 + half) * 4 + c] = acc[row : row + 4, c * 128 : (c + 1) * 128]


def sum_kernel(in_ref, out_ref):
    for c in range(3):
        total = in_ref[c]
        for p in range(1, PARTS):
            total = total + in_ref[3 * p + c]
        for p in range(PARTS):
            out_ref[3 * p + c] = total


def place_kernel(in_ref, self_ref, neigh_ref):
    for tile in range(12):
        for half in range(2):
            for c in range(4):
                value = in_ref[(tile * 2 + half) * 4 + c]
                row = (tile % 6) * 8 + half * 4
                ref = self_ref if tile < 6 else neigh_ref
                ref[row : row + 4, c * 128 : (c + 1) * 128] = value


def whole(shape):
    return pl.BlockSpec(shape, lambda *_: (0,) * len(shape))


def resident():
    return pl.BlockSpec(memory_space=pltpu.VMEM)


def exchange(x, axis):
    x = lax.all_to_all(x, axis, split_axis=0, concat_axis=0, tiled=True)
    return pltpu.with_memory_space_constraint(x, pltpu.VMEM)


def body(features, neighbors, degree, send_rows, labels, w_self, w_neigh, bias, a_self, a_neigh):
    degree = degree.reshape(1, NP)
    labels = labels.reshape(1, NP)
    bias, a_self, a_neigh = bias.reshape(1, HID), a_self.reshape(1, HID), a_neigh.reshape(1, HID)

    outgoing = call(send_kernel, sds((SENT, 128), BF16), "send")(features, send_rows)
    incoming = exchange(outgoing, "dom")

    steps = NP // WIDE
    nbr_spec = pl.BlockSpec((FAN, WIDE), lambda i: (0, i))
    deg_spec = pl.BlockSpec((1, WIDE), lambda i: (0, i))
    col_spec = pl.BlockSpec((SL, WIDE), lambda i: (0, i))
    own = call(
        own_kernel,
        sds((SL, NP), F32),
        "own",
        grid=(steps,),
        in_specs=[nbr_spec, deg_spec, whole((SL, NP))],
        out_specs=col_spec,
        scratch_shapes=[pltpu.VMEM((6 * OWN_FIELD, WIDE), BF16)],
    )(neighbors, degree, features)
    block = call(
        finish_kernel,
        sds((NB, 2 * SL, 128), BF16),
        "finish",
        grid=(steps,),
        in_specs=[resident(), nbr_spec, deg_spec, col_spec, col_spec],
        out_specs=pl.BlockSpec((WIDE // 128, 2 * SL, 128), lambda i: (i, 0, 0)),
        scratch_shapes=[pltpu.VMEM((6 * FAR_FIELD, WIDE), BF16), pltpu.VMEM((SL, SENT), BF16)],
    )(incoming, neighbors, degree, own, features)
    mine = exchange(block, "feat")

    mask, scores = call(preact_kernel, (sds((HID, 128), BF16), sds((NB, 8, 128), F32)), "preact")(
        mine, w_self, w_neigh, bias, a_self, a_neigh
    )
    scores = exchange(scores, "feat")
    mask, scores = lax.optimization_barrier((mask, scores))
    masks = lax.all_gather(mask, "feat", axis=0, tiled=False)
    score_out = call(boundary_score_kernel, sds((PARTS, 1, 128), F32), "bscore")(scores, send_rows)
    score_in = exchange(score_out, "dom")
    own_total = call(own_logit_kernel, sds((1, NP), F32), "ownlogit")(scores, neighbors, degree)

    logits, dlogit, slot, slot_out = call(
        logit_kernel,
        (sds((1, NP), F32), sds((1, NP), F32), sds((SLOTS // 128, 128), F32), sds((PARTS, 1, 128), F32)),
        "logit",
        scratch_shapes=[pltpu.VMEM((SENT // 128, 128), F32), pltpu.VMEM((3 * SLOTS // 128, 128), F32)],
    )(scores, own_total, score_in, neighbors, degree, labels)
    returned = exchange(slot_out, "dom")

    per = 4
    partial = call(
        grad_kernel,
        sds((96, 4, 128), F32),
        "grad",
        grid=(NB // per,),
        in_specs=[
            resident(),
            whole((1, B, PARTS)),
            whole((SLOTS // 128, 128)),
            whole((1, NP)),
            whole((1, HID)),
            whole((1, HID)),
            pl.BlockSpec((per, HID, 128), lambda i: (i, 0, 0)),
            pl.BlockSpec((per, 2 * SL, 128), lambda i: (i, 0, 0)),
        ],
        out_specs=whole((96, 4, 128)),
        scratch_shapes=[
            pltpu.VMEM((1, NP), F32),
            pltpu.VMEM((HID, 128), F32),
            pltpu.VMEM((HID, 128), F32),
            pltpu.VMEM((2 * SL, HID), F32),
        ],
    )(returned, send_rows, slot, dlogit, a_self, a_neigh, masks, block)
    shares = exchange(partial, "dom")
    summed = call(sum_kernel, sds((96, 4, 128), F32), "sum")(shares)
    summed = exchange(summed, "dom")
    grad_self, grad_neigh = call(place_kernel, (sds((SL, HID), F32), sds((SL, HID), F32)), "place")(summed)
    return (logits.reshape(NP), grad_self, grad_neigh)


def solution(mesh):
    return jax.shard_map(
        body,
        mesh=mesh,
        in_specs=(
            P("feat", "dom"),
            P(None, "dom"),
            P("dom"),
            P("dom", None, None),
            P("dom"),
            P(),
            P(),
            P(),
            P(),
            P(),
        ),
        out_specs=(P("dom"), P("feat", None), P("feat", None)),
        check_vma=False,
    )
```

```python
import jax
import jax.numpy as jnp
from jax import lax
from jax.experimental import pallas as pl
from jax.experimental.pallas import tpu as pltpu
from jax.sharding import PartitionSpec as P

F32 = jnp.float32
BF16 = jnp.bfloat16
I32 = jnp.int32

SL = 48
NP = 2048
NB = 16
PARTS = 32
B = 32
SENT = 1024
SLOTS = 3072
FAN = 16
HID = 512
OWN_FIELD = 352
FAR_FIELD = 176


def call(kernel, out_shape, name, **kw):
    return pl.pallas_call(kernel, out_shape=out_shape, name=name, **kw)


def sds(shape, dtype):
    return jax.ShapeDtypeStruct(shape, dtype)


def split3(x):
    hi = x.astype(BF16)
    rest = x - hi.astype(F32)
    mid = rest.astype(BF16)
    low = (rest - mid.astype(F32)).astype(BF16)
    return hi, mid, low


def send_kernel(feat_ref, send_ref, out_ref):
    feats = feat_ref[...]
    columns = jnp.transpose(send_ref[0], (1, 0))
    lanes = lax.broadcasted_iota(I32, (B, NP), 1)
    out_ref[...] = jnp.zeros_like(out_ref)
    for r in range(PARTS // 4):
        onehot = jnp.concatenate(
            [jnp.where(columns[:, p : p + 1] == lanes, 1.0, 0.0).astype(BF16) for p in range(4 * r, 4 * r + 4)], axis=0
        )
        rows = lax.dot_general(onehot, feats, (((1,), (1,)), ((), ())), preferred_element_type=F32)
        out_ref[pl.ds(r * 128, 128), 0:SL] = rows.astype(BF16)


def build_counts(nbr_ref, deg_ref, cnt_ref, lanes, first, size, field):
    rows8 = lax.broadcasted_iota(I32, (8, 128), 0)
    idx = nbr_ref[:, lanes] - first
    valid = (lax.broadcasted_iota(I32, (FAN, 128), 0) < deg_ref[:, lanes]) & (idx >= 0) & (idx < size)
    which = jnp.zeros_like(idx)
    for j in range(1, 6):
        which = which + jnp.where(idx >= j * field, 1, 0)
    q = jnp.where(valid, idx - which * field, -1)
    v = jnp.left_shift(jnp.ones_like(idx), which * 5)
    qs = [jnp.broadcast_to(q[k : k + 1], (8, 128)) for k in range(FAN)]
    vs = [jnp.broadcast_to(v[k : k + 1], (8, 128)) for k in range(FAN)]
    for base in range(0, field, 16):
        packed = []
        for part in range(2):
            t = rows8 + (base + 8 * part)
            acc = jnp.zeros((8, 128), I32)
            for k in range(FAN):
                acc = acc + jnp.where(qs[k] == t, vs[k], 0)
            packed.append(acc)
        both = jnp.concatenate(packed, axis=0)
        for j in range(6):
            count = jnp.bitwise_and(lax.shift_right_logical(both, 5 * j), 31)
            cnt_ref[j * field + base : j * field + base + 16, :] = count.astype(F32).astype(BF16)


def pipelined(nbr_ref, deg_ref, buffers, first, size, field, multiply):
    def lanes(n):
        return pl.ds(pl.multiple_of(n * 128, 128), 128)

    def pair(n, carry):
        multiply(jnp.maximum(2 * n - 1, 0), buffers[1])
        build_counts(nbr_ref, deg_ref, buffers[0], lanes(2 * n), first, size, field)
        multiply(2 * n, buffers[0])
        build_counts(nbr_ref, deg_ref, buffers[1], lanes(2 * n + 1), first, size, field)
        return carry

    lax.fori_loop(0, NB // 2, pair, 0)
    multiply(NB - 1, buffers[1])


def own_kernel(nbr_ref, deg_ref, feat_ref, own_ref, cnt0, cnt1):
    def multiply(n, cnt):
        own_ref[n] = jnp.dot(feat_ref[...], cnt[0:NP, :], preferred_element_type=F32)

    pipelined(nbr_ref, deg_ref, (cnt0, cnt1), 0, NP, OWN_FIELD, multiply)


def finish_kernel(recv_ref, nbr_ref, deg_ref, own_ref, feat_ref, out_ref, cnt0, cnt1, recv):
    recv[...] = jnp.transpose(recv_ref[...].astype(F32), (1, 0))[0:SL].astype(BF16)

    def multiply(n, cnt):
        lanes = pl.ds(pl.multiple_of(n * 128, 128), 128)
        far = jnp.dot(recv[...], cnt[0:SENT, :], preferred_element_type=F32)
        inverse = 1.0 / deg_ref[:, lanes].astype(F32)
        out_ref[n, 0:SL, :] = feat_ref[:, lanes]
        out_ref[n, SL : 2 * SL, :] = ((own_ref[n] + far) * inverse).astype(BF16)

    pipelined(nbr_ref, deg_ref, (cnt0, cnt1), NP, SENT, FAR_FIELD, multiply)


def columns(*refs):
    rows = [ref[...] for ref in refs] + [jnp.zeros((8 - len(refs), HID), F32)]
    return jnp.transpose(jnp.concatenate(rows, axis=0), (1, 0))


def preact_kernel(block_ref, ws_ref, wn_ref, bias_ref, as_ref, an_ref, mask_ref, score_ref):
    dims = (((0,), (0,)), ((), ()))
    pre = lax.dot_general(block_ref[:, 0:SL, :].reshape(SL * NB, 128), ws_ref[...], dims, preferred_element_type=F32)
    pre = pre + lax.dot_general(block_ref[:, SL : 2 * SL, :].reshape(SL * NB, 128), wn_ref[...], dims, preferred_element_type=F32)
    par = columns(bias_ref, as_ref, an_ref)
    pre = jnp.transpose(pre, (1, 0)) + par[:, 0:1]
    hidden = jnp.maximum(pre, 0.0)
    mask_ref[...] = jnp.where(pre > 0, 1.0, 0.0).astype(BF16)
    own = jnp.sum(hidden * par[:, 1:2], axis=0, keepdims=True)
    neigh = jnp.sum(hidden * par[:, 2:3], axis=0, keepdims=True)
    both = jnp.concatenate([own, neigh, jnp.zeros((6, 128), F32)], axis=0)
    for b in range(NB):
        score_ref[b] = both


def lane_gather(row, idx):
    return jnp.take_along_axis(jnp.broadcast_to(row, idx.shape), idx, axis=1)


def boundary_score_kernel(score_ref, send_ref, out_ref):
    idx = jnp.concatenate([send_ref[0], jnp.zeros((PARTS, 96), I32)], axis=1)
    low = jnp.bitwise_and(idx, 127)
    high = lax.shift_right_logical(idx, 7)
    acc = jnp.zeros((PARTS, 128), F32)
    for b in range(NB):
        acc = jnp.where(high == b, lane_gather(score_ref[b, 1:2, :], low), acc)
    for p in range(PARTS):
        out_ref[p] = acc[p : p + 1, :]


def own_logit_kernel(score_ref, nbr_ref, deg_ref, out_ref):
    def one(f, carry):
        lanes = pl.ds(pl.multiple_of(f * 128, 128), 128)
        idx = nbr_ref[:, lanes]
        low = jnp.bitwise_and(idx, 127)
        high = lax.shift_right_logical(idx, 7)
        acc = jnp.zeros((FAN, 128), F32)
        for r in range(NB):
            acc = jnp.where(high == r, lane_gather(score_ref[r, 1:2, :], low), acc)
        valid = lax.broadcasted_iota(I32, (FAN, 128), 0) < deg_ref[:, lanes]
        out_ref[:, lanes] = jnp.sum(jnp.where(valid, acc, 0.0), axis=0, keepdims=True)
        return carry

    lax.fori_loop(0, NB, one, 0)


def dense_rows(ref):
    lane = lax.broadcasted_iota(I32, (8, 128), 1)
    acc = jnp.zeros((8, 128), F32)
    for g in range(4):
        rows = jnp.concatenate([ref[4 * r + g] for r in range(8)], axis=0)
        rows = pltpu.roll(rows, 32 * g, 1) if g else rows
        acc = jnp.where(lax.shift_right_logical(lane, 5) == g, rows, acc)
    return acc


def logit_kernel(score_ref, own_ref, far_ref, nbr_ref, deg_ref, label_ref, logit_ref, dlogit_ref, slot_ref, out_ref, table, acc_ref):
    table[...] = dense_rows(far_ref)
    acc_ref[...] = jnp.zeros_like(acc_ref)
    highs = SLOTS // 128
    high_rows = lax.broadcasted_iota(I32, (highs, 128), 0)
    low_rows = lax.broadcasted_iota(I32, (16, 128), 0)
    one16, zero16 = jnp.ones((16, 128), BF16), jnp.zeros((16, 128), BF16)

    def one(f, left, right):
        lanes = pl.ds(pl.multiple_of(f * 128, 128), 128)
        idx = nbr_ref[:, lanes]
        low = jnp.bitwise_and(idx, 127)
        high = lax.shift_right_logical(idx, 7)
        acc = jnp.zeros((FAN, 128), F32)
        for r in range(SENT // 128):
            acc = jnp.where(high == NB + r, lane_gather(table[r : r + 1, :], low), acc)
        degree = deg_ref[:, lanes]
        valid = lax.broadcasted_iota(I32, (FAN, 128), 0) < degree
        inverse = 1.0 / degree.astype(F32)
        total = own_ref[:, lanes] + jnp.sum(jnp.where(valid, acc, 0.0), axis=0, keepdims=True)
        logits = score_ref[f, 0:1, :] + total * inverse
        logit_ref[:, lanes] = logits
        dlogit = (jax.nn.sigmoid(logits) - label_ref[:, lanes].astype(F32)) * (float(NP * PARTS) ** -0.5)
        dlogit_ref[:, lanes] = dlogit
        thirds = [t.astype(F32) for t in split3(dlogit * inverse)]
        high = jnp.where(valid, high, -1)
        for k in range(FAN):
            hit = high[k : k + 1] == high_rows
            left.append(jnp.concatenate([jnp.where(hit, t, 0.0) for t in thirds], axis=0).astype(BF16))
            offset = (jnp.broadcast_to(low[k : k + 1], (16, 128)) - low_rows).astype(F32).astype(BF16)
            right.append(jnp.concatenate([jnp.where(offset == 16.0 * j, one16, zero16) for j in range(8)], axis=0))

    def pair(n, carry):
        left, right = [], []
        one(2 * n, left, right)
        one(2 * n + 1, left, right)
        acc_ref[...] += lax.dot_general(
            jnp.concatenate(left, axis=1),
            jnp.concatenate(right, axis=1),
            (((1,), (1,)), ((), ())),
            preferred_element_type=F32,
        )
        return carry

    lax.fori_loop(0, NB // 2, pair, 0)
    slot = acc_ref[0:highs] + acc_ref[highs : 2 * highs] + acc_ref[2 * highs : 3 * highs]
    slot_ref[...] = slot
    for r in range(8):
        row = slot[NB + r : NB + r + 1, :]
        for g in range(4):
            out_ref[4 * r + g] = pltpu.roll(row, 128 - 32 * g, 1) if g else row


def grad_kernel(ret_ref, send_ref, slot_ref, dlogit_ref, as_ref, an_ref, mask_ref, block_ref, out_ref, dneigh, wide_s, wide_n, acc):
    step = pl.program_id(0)
    per = mask_ref.shape[0]

    @pl.when(step == 0)
    def _():
        send = jnp.transpose(send_ref[0], (1, 0))
        back = jnp.transpose(jnp.concatenate([ret_ref[p] for p in range(PARTS)], axis=0), (1, 0))[0:B]
        lane = lax.broadcasted_iota(I32, (8, 128), 1)
        totals = [jnp.zeros((8, 128), F32) for _ in range(NB)]
        for p in range(PARTS):
            for c in range(B // 8):
                node = jnp.broadcast_to(send[8 * c : 8 * c + 8, p : p + 1], (8, 128)) - lane
                value = jnp.broadcast_to(back[8 * c : 8 * c + 8, p : p + 1], (8, 128))
                for f in range(NB):
                    totals[f] = totals[f] + jnp.where(node == f * 128, value, 0.0)
        for f in range(NB):
            lanes = slice(f * 128, (f + 1) * 128)
            dneigh[:, lanes] = slot_ref[f : f + 1, :] + jnp.sum(totals[f], axis=0, keepdims=True)
        par = columns(as_ref, an_ref)
        wide_s[...] = jnp.broadcast_to(par[:, 0:1], (HID, 128))
        wide_n[...] = jnp.broadcast_to(par[:, 1:2], (HID, 128))
        acc[...] = jnp.zeros_like(acc)

    for b in range(per):
        lanes = pl.ds(pl.multiple_of((step * per + b) * 128, 128), 128)
        grad = wide_s[...] * dlogit_ref[:, lanes] + wide_n[...] * dneigh[:, lanes]
        dpre = grad.astype(BF16) * mask_ref[b]
        acc[...] += lax.dot_general(block_ref[b], dpre, (((1,), (1,)), ((), ())), preferred_element_type=F32)

    @pl.when(step == pl.num_programs(0) - 1)
    def _():
        for tile in range(12):
            for half in range(2):
                for c in range(4):
                    row = tile * 8 + half * 4
                    out_ref[(tile * 2 + half) * 4 + c] = acc[row : row + 4, c * 128 : (c + 1) * 128].astype(BF16)


def sum_kernel(in_ref, out_ref):
    for c in range(3):
        total = in_ref[c].astype(F32)
        for p in range(1, PARTS):
            total = total + in_ref[3 * p + c].astype(F32)
        total = total.astype(BF16)
        for p in range(PARTS):
            out_ref[3 * p + c] = total


def place_kernel(in_ref, self_ref, neigh_ref):
    for tile in range(12):
        for half in range(2):
            for c in range(4):
                value = in_ref[(tile * 2 + half) * 4 + c].astype(F32)
                row = (tile % 6) * 8 + half * 4
                ref = self_ref if tile < 6 else neigh_ref
                ref[row : row + 4, c * 128 : (c + 1) * 128] = value


def whole(shape):
    return pl.BlockSpec(shape, lambda *_: (0,) * len(shape))


def resident():
    return pl.BlockSpec(memory_space=pltpu.VMEM)


def exchange(x, axis):
    x = lax.all_to_all(x, axis, split_axis=0, concat_axis=0, tiled=True)
    return pltpu.with_memory_space_constraint(x, pltpu.VMEM)


def body(features, neighbors, degree, send_rows, labels, w_self, w_neigh, bias, a_self, a_neigh):
    degree = degree.reshape(1, NP)
    labels = labels.reshape(1, NP)
    bias, a_self, a_neigh = bias.reshape(1, HID), a_self.reshape(1, HID), a_neigh.reshape(1, HID)

    outgoing = call(send_kernel, sds((SENT, 128), BF16), "send")(features, send_rows)
    incoming = exchange(outgoing, "dom")

    own = call(
        own_kernel,
        sds((NB, SL, 128), F32),
        "own",
        scratch_shapes=[pltpu.VMEM((6 * OWN_FIELD, 128), BF16)] * 2,
    )(neighbors, degree, features)
    block = call(
        finish_kernel,
        sds((NB, 2 * SL, 128), BF16),
        "finish",
        scratch_shapes=[pltpu.VMEM((6 * FAR_FIELD, 128), BF16)] * 2 + [pltpu.VMEM((SL, SENT), BF16)],
    )(incoming, neighbors, degree, own, features)
    mine = exchange(block, "feat")

    mask, scores = call(preact_kernel, (sds((HID, 128), BF16), sds((NB, 8, 128), F32)), "preact")(
        mine, w_self, w_neigh, bias, a_self, a_neigh
    )
    scores = exchange(scores, "feat")
    mask, scores = lax.optimization_barrier((mask, scores))
    masks = lax.all_gather(mask, "feat", axis=0, tiled=False)
    score_out = call(boundary_score_kernel, sds((PARTS, 1, 128), F32), "bscore")(scores, send_rows)
    score_in = exchange(score_out, "dom")
    own_total = call(own_logit_kernel, sds((1, NP), F32), "ownlogit")(scores, neighbors, degree)

    logits, dlogit, slot, slot_out = call(
        logit_kernel,
        (sds((1, NP), F32), sds((1, NP), F32), sds((SLOTS // 128, 128), F32), sds((PARTS, 1, 128), F32)),
        "logit",
        scratch_shapes=[pltpu.VMEM((SENT // 128, 128), F32), pltpu.VMEM((3 * SLOTS // 128, 128), F32)],
    )(scores, own_total, score_in, neighbors, degree, labels)
    returned = exchange(slot_out, "dom")

    per = 4
    partial = call(
        grad_kernel,
        sds((96, 4, 128), BF16),
        "grad",
        grid=(NB // per,),
        in_specs=[
            resident(),
            whole((1, B, PARTS)),
            whole((SLOTS // 128, 128)),
            whole((1, NP)),
            whole((1, HID)),
            whole((1, HID)),
            pl.BlockSpec((per, HID, 128), lambda i: (i, 0, 0)),
            pl.BlockSpec((per, 2 * SL, 128), lambda i: (i, 0, 0)),
        ],
        out_specs=whole((96, 4, 128)),
        scratch_shapes=[
            pltpu.VMEM((1, NP), F32),
            pltpu.VMEM((HID, 128), F32),
            pltpu.VMEM((HID, 128), F32),
            pltpu.VMEM((2 * SL, HID), F32),
        ],
    )(returned, send_rows, slot, dlogit, a_self, a_neigh, masks, block)
    shares = exchange(partial, "dom")
    summed = call(sum_kernel, sds((96, 4, 128), BF16), "sum")(shares)
    summed = exchange(summed, "dom")
    grad_self, grad_neigh = call(place_kernel, (sds((SL, HID), F32), sds((SL, HID), F32)), "place")(summed)
    return (logits.reshape(NP), grad_self, grad_neigh)


def solution(mesh):
    return jax.shard_map(
        body,
        mesh=mesh,
        in_specs=(
            P("feat", "dom"),
            P(None, "dom"),
            P("dom"),
            P("dom", None, None),
            P("dom"),
            P(),
            P(),
            P(),
            P(),
            P(),
        ),
        out_specs=(P("dom"), P("feat", None), P("feat", None)),
        check_vma=False,
    )
```

```python
import jax
import jax.numpy as jnp
from jax import lax
from jax.experimental import pallas as pl
from jax.experimental.pallas import tpu as pltpu
from jax.sharding import PartitionSpec as P

F32 = jnp.float32
BF16 = jnp.bfloat16
I32 = jnp.int32

SL = 48
NP = 2048
NB = 16
PARTS = 32
B = 32
SENT = 1024
SLOTS = 3072
FAN = 16
HID = 512
OWN_FIELD = 352
FAR_FIELD = 176


def call(kernel, out_shape, name, **kw):
    return pl.pallas_call(kernel, out_shape=out_shape, name=name, **kw)


def sds(shape, dtype):
    return jax.ShapeDtypeStruct(shape, dtype)


def split3(x):
    hi = x.astype(BF16)
    rest = x - hi.astype(F32)
    mid = rest.astype(BF16)
    low = (rest - mid.astype(F32)).astype(BF16)
    return hi, mid, low


def send_kernel(feat_ref, send_ref, out_ref):
    feats = feat_ref[...]
    columns = jnp.transpose(send_ref[0], (1, 0))
    lanes = lax.broadcasted_iota(I32, (B, NP), 1)
    out_ref[...] = jnp.zeros_like(out_ref)
    for r in range(PARTS // 4):
        onehot = jnp.concatenate(
            [jnp.where(columns[:, p : p + 1] == lanes, 1.0, 0.0).astype(BF16) for p in range(4 * r, 4 * r + 4)], axis=0
        )
        rows = lax.dot_general(onehot, feats, (((1,), (1,)), ((), ())), preferred_element_type=F32)
        out_ref[pl.ds(r * 128, 128), 0:SL] = rows.astype(BF16)


def build_counts(nbr_ref, deg_ref, cnt_ref, lanes, first, size, field, group):
    rows8 = lax.broadcasted_iota(I32, (8, 128), 0)
    idx = nbr_ref[:, lanes] - first
    valid = (lax.broadcasted_iota(I32, (FAN, 128), 0) < deg_ref[:, lanes]) & (idx >= 0) & (idx < size)
    which = jnp.zeros_like(idx)
    for j in range(1, 6):
        which = which + jnp.where(idx >= j * field, 1, 0)
    q = idx - which * field
    v = jnp.left_shift(jnp.ones_like(idx), which * 5)
    above = jnp.where(valid, lax.shift_right_arithmetic(q, group.bit_length() - 1), -1)
    below = jnp.bitwise_and(q, group - 1)
    aboves, tables = [], []
    for k in range(FAN):
        aboves.append(jnp.broadcast_to(above[k : k + 1], (8, 128)))
        low = jnp.broadcast_to(below[k : k + 1], (8, 128))
        value = jnp.broadcast_to(v[k : k + 1], (8, 128))
        tables.append([jnp.where(low == rows8 + 8 * c, value, 0) for c in range(group // 8)])
    for g in range(field // group):
        accs = [jnp.zeros((8, 128), I32)] * (group // 8)
        for k in range(FAN):
            hit = aboves[k] == g
            accs = [acc + jnp.where(hit, tables[k][c], 0) for c, acc in enumerate(accs)]
        for c in range(0, group // 8, 2):
            both = jnp.concatenate(accs[c : c + 2], axis=0)
            for j in range(6):
                count = jnp.bitwise_and(both, 31 << (5 * j)).astype(F32).astype(BF16)
                row = j * field + g * group + 8 * c
                cnt_ref[row : row + 16, :] = count


def scaled(values, field):
    slot = lax.broadcasted_iota(I32, values.shape, 1)
    scale = jnp.full(values.shape, 2.0**12, F32)
    for j in range(1, 6):
        scale = jnp.where(slot >= j * field, 2.0 ** (12 - 5 * j), scale)
    return (values.astype(F32) * scale).astype(BF16)


def pipelined(nbr_ref, deg_ref, buffers, first, size, field, group, multiply):
    def lanes(n):
        return pl.ds(pl.multiple_of(n * 128, 128), 128)

    def pair(n, carry):
        multiply(jnp.maximum(2 * n - 1, 0), buffers[1])
        build_counts(nbr_ref, deg_ref, buffers[0], lanes(2 * n), first, size, field, group)
        multiply(2 * n, buffers[0])
        build_counts(nbr_ref, deg_ref, buffers[1], lanes(2 * n + 1), first, size, field, group)
        return carry

    lax.fori_loop(0, NB // 2, pair, 0)
    multiply(NB - 1, buffers[1])


def own_kernel(nbr_ref, deg_ref, feat_ref, own_ref, cnt0, cnt1, feats):
    feats[...] = scaled(feat_ref[...], OWN_FIELD)

    def multiply(n, cnt):
        own_ref[n] = jnp.dot(feats[...], cnt[0:NP, :], preferred_element_type=F32)

    pipelined(nbr_ref, deg_ref, (cnt0, cnt1), 0, NP, OWN_FIELD, 32, multiply)


def finish_kernel(recv_ref, nbr_ref, deg_ref, own_ref, feat_ref, out_ref, cnt0, cnt1, recv):
    recv[...] = scaled(jnp.transpose(recv_ref[...].astype(F32), (1, 0))[0:SL], FAR_FIELD)

    def multiply(n, cnt):
        lanes = pl.ds(pl.multiple_of(n * 128, 128), 128)
        far = jnp.dot(recv[...], cnt[0:SENT, :], preferred_element_type=F32)
        inverse = 1.0 / deg_ref[:, lanes].astype(F32)
        out_ref[n, 0:SL, :] = feat_ref[:, lanes]
        out_ref[n, SL : 2 * SL, :] = ((own_ref[n] + far) * 2.0**-12 * inverse).astype(BF16)

    pipelined(nbr_ref, deg_ref, (cnt0, cnt1), NP, SENT, FAR_FIELD, 16, multiply)


def columns(*refs):
    rows = [ref[...] for ref in refs] + [jnp.zeros((8 - len(refs), HID), F32)]
    return jnp.transpose(jnp.concatenate(rows, axis=0), (1, 0))


def preact_kernel(block_ref, ws_ref, wn_ref, bias_ref, as_ref, an_ref, mask_ref, score_ref):
    dims = (((0,), (0,)), ((), ()))
    pre = lax.dot_general(block_ref[:, 0:SL, :].reshape(SL * NB, 128), ws_ref[...], dims, preferred_element_type=F32)
    pre = pre + lax.dot_general(block_ref[:, SL : 2 * SL, :].reshape(SL * NB, 128), wn_ref[...], dims, preferred_element_type=F32)
    par = columns(bias_ref, as_ref, an_ref)
    pre = jnp.transpose(pre, (1, 0)) + par[:, 0:1]
    hidden = jnp.maximum(pre, 0.0)
    mask_ref[...] = jnp.where(pre > 0, 1.0, 0.0).astype(BF16)
    own = jnp.sum(hidden * par[:, 1:2], axis=0, keepdims=True)
    neigh = jnp.sum(hidden * par[:, 2:3], axis=0, keepdims=True)
    both = jnp.concatenate([own, neigh, jnp.zeros((6, 128), F32)], axis=0)
    for b in range(NB):
        score_ref[b] = both


def lane_gather(row, idx):
    return jnp.take_along_axis(jnp.broadcast_to(row, idx.shape), idx, axis=1)


def boundary_score_kernel(score_ref, send_ref, out_ref):
    idx = jnp.concatenate([send_ref[0], jnp.zeros((PARTS, 96), I32)], axis=1)
    low = jnp.bitwise_and(idx, 127)
    high = lax.shift_right_logical(idx, 7)
    acc = jnp.zeros((PARTS, 128), F32)
    for b in range(NB):
        acc = jnp.where(high == b, lane_gather(score_ref[b, 1:2, :], low), acc)
    for p in range(PARTS):
        out_ref[p] = acc[p : p + 1, :]


def own_logit_kernel(score_ref, nbr_ref, deg_ref, out_ref):
    def one(f, carry):
        lanes = pl.ds(pl.multiple_of(f * 128, 128), 128)
        idx = nbr_ref[:, lanes]
        low = jnp.bitwise_and(idx, 127)
        high = lax.shift_right_logical(idx, 7)
        acc = jnp.zeros((FAN, 128), F32)
        for r in range(NB):
            acc = jnp.where(high == r, lane_gather(score_ref[r, 1:2, :], low), acc)
        valid = lax.broadcasted_iota(I32, (FAN, 128), 0) < deg_ref[:, lanes]
        out_ref[:, lanes] = jnp.sum(jnp.where(valid, acc, 0.0), axis=0, keepdims=True)
        return carry

    lax.fori_loop(0, NB, one, 0)


def dense_rows(ref):
    lane = lax.broadcasted_iota(I32, (8, 128), 1)
    acc = jnp.zeros((8, 128), F32)
    for g in range(4):
        rows = jnp.concatenate([ref[4 * r + g] for r in range(8)], axis=0)
        rows = pltpu.roll(rows, 32 * g, 1) if g else rows
        acc = jnp.where(lax.shift_right_logical(lane, 5) == g, rows, acc)
    return acc


def logit_kernel(score_ref, own_ref, far_ref, nbr_ref, deg_ref, label_ref, logit_ref, dlogit_ref, slot_ref, out_ref, table, acc_ref):
    table[...] = dense_rows(far_ref)
    acc_ref[...] = jnp.zeros_like(acc_ref)
    highs = SLOTS // 128
    high_rows = lax.broadcasted_iota(I32, (highs, 128), 0)
    low_rows = lax.broadcasted_iota(I32, (16, 128), 0)
    one16, zero16 = jnp.ones((16, 128), BF16), jnp.zeros((16, 128), BF16)

    def one(f, left, right):
        lanes = pl.ds(pl.multiple_of(f * 128, 128), 128)
        idx = nbr_ref[:, lanes]
        low = jnp.bitwise_and(idx, 127)
        high = lax.shift_right_logical(idx, 7)
        acc = jnp.zeros((FAN, 128), F32)
        for r in range(SENT // 128):
            acc = jnp.where(high == NB + r, lane_gather(table[r : r + 1, :], low), acc)
        degree = deg_ref[:, lanes]
        valid = lax.broadcasted_iota(I32, (FAN, 128), 0) < degree
        inverse = 1.0 / degree.astype(F32)
        total = own_ref[:, lanes] + jnp.sum(jnp.where(valid, acc, 0.0), axis=0, keepdims=True)
        logits = score_ref[f, 0:1, :] + total * inverse
        logit_ref[:, lanes] = logits
        dlogit = (jax.nn.sigmoid(logits) - label_ref[:, lanes].astype(F32)) * (float(NP * PARTS) ** -0.5)
        dlogit_ref[:, lanes] = dlogit
        thirds = [t.astype(F32) for t in split3(dlogit * inverse)]
        high = jnp.where(valid, high, -1)
        for k in range(FAN):
            hit = high[k : k + 1] == high_rows
            left.append(jnp.concatenate([jnp.where(hit, t, 0.0) for t in thirds], axis=0).astype(BF16))
            offset = (jnp.broadcast_to(low[k : k + 1], (16, 128)) - low_rows).astype(F32).astype(BF16)
            right.append(jnp.concatenate([jnp.where(offset == 16.0 * j, one16, zero16) for j in range(8)], axis=0))

    def pair(n, carry):
        left, right = [], []
        one(2 * n, left, right)
        one(2 * n + 1, left, right)
        acc_ref[...] += lax.dot_general(
            jnp.concatenate(left, axis=1),
            jnp.concatenate(right, axis=1),
            (((1,), (1,)), ((), ())),
            preferred_element_type=F32,
        )
        return carry

    lax.fori_loop(0, NB // 2, pair, 0)
    slot = acc_ref[0:highs] + acc_ref[highs : 2 * highs] + acc_ref[2 * highs : 3 * highs]
    slot_ref[...] = slot
    for r in range(8):
        row = slot[NB + r : NB + r + 1, :]
        for g in range(4):
            out_ref[4 * r + g] = pltpu.roll(row, 128 - 32 * g, 1) if g else row


def grad_kernel(ret_ref, send_ref, slot_ref, dlogit_ref, as_ref, an_ref, mask_ref, block_ref, out_ref, dneigh, wide_s, wide_n, acc):
    step = pl.program_id(0)
    per = mask_ref.shape[0]

    @pl.when(step == 0)
    def _():
        send = jnp.transpose(send_ref[0], (1, 0))
        back = jnp.transpose(jnp.concatenate([ret_ref[p] for p in range(PARTS)], axis=0), (1, 0))[0:B]
        lane = lax.broadcasted_iota(I32, (8, 128), 1)
        totals = [jnp.zeros((8, 128), F32) for _ in range(NB)]
        for p in range(PARTS):
            for c in range(B // 8):
                node = jnp.broadcast_to(send[8 * c : 8 * c + 8, p : p + 1], (8, 128)) - lane
                value = jnp.broadcast_to(back[8 * c : 8 * c + 8, p : p + 1], (8, 128))
                for f in range(NB):
                    totals[f] = totals[f] + jnp.where(node == f * 128, value, 0.0)
        for f in range(NB):
            lanes = slice(f * 128, (f + 1) * 128)
            dneigh[:, lanes] = slot_ref[f : f + 1, :] + jnp.sum(totals[f], axis=0, keepdims=True)
        par = columns(as_ref, an_ref)
        wide_s[...] = jnp.broadcast_to(par[:, 0:1], (HID, 128))
        wide_n[...] = jnp.broadcast_to(par[:, 1:2], (HID, 128))
        acc[...] = jnp.zeros_like(acc)

    for b in range(per):
        lanes = pl.ds(pl.multiple_of((step * per + b) * 128, 128), 128)
        grad = wide_s[...] * dlogit_ref[:, lanes] + wide_n[...] * dneigh[:, lanes]
        dpre = grad.astype(BF16) * mask_ref[b]
        acc[...] += lax.dot_general(block_ref[b], dpre, (((1,), (1,)), ((), ())), preferred_element_type=F32)

    @pl.when(step == pl.num_programs(0) - 1)
    def _():
        for tile in range(12):
            for half in range(2):
                for c in range(4):
                    row = tile * 8 + half * 4
                    out_ref[(tile * 2 + half) * 4 + c] = acc[row : row + 4, c * 128 : (c + 1) * 128].astype(BF16)


def sum_kernel(in_ref, out_ref):
    for c in range(3):
        total = in_ref[c].astype(F32)
        for p in range(1, PARTS):
            total = total + in_ref[3 * p + c].astype(F32)
        total = total.astype(BF16)
        for p in range(PARTS):
            out_ref[3 * p + c] = total


def place_kernel(in_ref, self_ref, neigh_ref):
    for tile in range(12):
        for half in range(2):
            for c in range(4):
                value = in_ref[(tile * 2 + half) * 4 + c].astype(F32)
                row = (tile % 6) * 8 + half * 4
                ref = self_ref if tile < 6 else neigh_ref
                ref[row : row + 4, c * 128 : (c + 1) * 128] = value


def whole(shape):
    return pl.BlockSpec(shape, lambda *_: (0,) * len(shape))


def resident():
    return pl.BlockSpec(memory_space=pltpu.VMEM)


def near(x):
    return pltpu.with_memory_space_constraint(x, pltpu.VMEM)


def exchange(x, axis):
    return near(lax.all_to_all(x, axis, split_axis=0, concat_axis=0, tiled=True))


def body(features, neighbors, degree, send_rows, labels, w_self, w_neigh, bias, a_self, a_neigh):
    degree = degree.reshape(1, NP)
    labels = labels.reshape(1, NP)
    bias, a_self, a_neigh = bias.reshape(1, HID), a_self.reshape(1, HID), a_neigh.reshape(1, HID)

    outgoing = call(send_kernel, sds((SENT, 128), BF16), "send")(features, send_rows)
    incoming = exchange(outgoing, "dom")

    own = call(
        own_kernel,
        sds((NB, SL, 128), F32),
        "own",
        scratch_shapes=[pltpu.VMEM((6 * OWN_FIELD, 128), BF16)] * 2 + [pltpu.VMEM((SL, NP), BF16)],
    )(neighbors, degree, features)
    block = call(
        finish_kernel,
        sds((NB, 2 * SL, 128), BF16),
        "finish",
        scratch_shapes=[pltpu.VMEM((6 * FAR_FIELD, 128), BF16)] * 2 + [pltpu.VMEM((SL, SENT), BF16)],
    )(incoming, neighbors, degree, own, features)
    mine = exchange(block, "feat")

    mask, scores = call(preact_kernel, (sds((HID, 128), BF16), sds((NB, 8, 128), F32)), "preact")(
        mine, near(w_self), near(w_neigh), bias, a_self, a_neigh
    )
    scores = exchange(scores, "feat")
    mask, scores = lax.optimization_barrier((mask, scores))
    masks = lax.all_gather(mask, "feat", axis=0, tiled=False)
    score_out = call(boundary_score_kernel, sds((PARTS, 1, 128), F32), "bscore")(scores, send_rows)
    score_in = exchange(score_out, "dom")
    own_total = call(own_logit_kernel, sds((1, NP), F32), "ownlogit")(scores, neighbors, degree)

    logits, dlogit, slot, slot_out = call(
        logit_kernel,
        (sds((1, NP), F32), sds((1, NP), F32), sds((SLOTS // 128, 128), F32), sds((PARTS, 1, 128), F32)),
        "logit",
        scratch_shapes=[pltpu.VMEM((SENT // 128, 128), F32), pltpu.VMEM((3 * SLOTS // 128, 128), F32)],
    )(scores, own_total, score_in, neighbors, degree, labels)
    returned = exchange(slot_out, "dom")

    per = 4
    partial = call(
        grad_kernel,
        sds((96, 4, 128), BF16),
        "grad",
        grid=(NB // per,),
        in_specs=[
            resident(),
            whole((1, B, PARTS)),
            whole((SLOTS // 128, 128)),
            whole((1, NP)),
            whole((1, HID)),
            whole((1, HID)),
            pl.BlockSpec((per, HID, 128), lambda i: (i, 0, 0)),
            pl.BlockSpec((per, 2 * SL, 128), lambda i: (i, 0, 0)),
        ],
        out_specs=whole((96, 4, 128)),
        scratch_shapes=[
            pltpu.VMEM((1, NP), F32),
            pltpu.VMEM((HID, 128), F32),
            pltpu.VMEM((HID, 128), F32),
            pltpu.VMEM((2 * SL, HID), F32),
        ],
    )(returned, send_rows, slot, dlogit, a_self, a_neigh, masks, block)
    shares = exchange(partial, "dom")
    summed = call(sum_kernel, sds((96, 4, 128), BF16), "sum")(shares)
    summed = exchange(summed, "dom")
    grad_self, grad_neigh = call(place_kernel, (sds((SL, HID), F32), sds((SL, HID), F32)), "place")(summed)
    return (logits.reshape(NP), grad_self, grad_neigh)


def solution(mesh):
    return jax.shard_map(
        body,
        mesh=mesh,
        in_specs=(
            P("feat", "dom"),
            P(None, "dom"),
            P("dom"),
            P("dom", None, None),
            P("dom"),
            P(),
            P(),
            P(),
            P(),
            P(),
        ),
        out_specs=(P("dom"), P("feat", None), P("feat", None)),
        check_vma=False,
    )
```

```python
import jax
import jax.numpy as jnp
from jax import lax
from jax.experimental import pallas as pl
from jax.experimental.pallas import tpu as pltpu
from jax.sharding import PartitionSpec as P

F32 = jnp.float32
BF16 = jnp.bfloat16
I32 = jnp.int32

SL = 48
NP = 2048
NB = 16
PARTS = 32
B = 32
SENT = 1024
SLOTS = 3072
FAN = 16
HID = 512
OWN_FIELD = 352
FAR_FIELD = 176


def call(kernel, out_shape, name, **kw):
    return pl.pallas_call(kernel, out_shape=out_shape, name=name, **kw)


def sds(shape, dtype):
    return jax.ShapeDtypeStruct(shape, dtype)


def split3(x):
    hi = x.astype(BF16)
    rest = x - hi.astype(F32)
    mid = rest.astype(BF16)
    low = (rest - mid.astype(F32)).astype(BF16)
    return hi, mid, low


def send_kernel(feat_ref, send_ref, out_ref):
    feats = feat_ref[...]
    columns = jnp.transpose(send_ref[0], (1, 0))
    lanes = lax.broadcasted_iota(I32, (B, NP), 1)
    out_ref[...] = jnp.zeros_like(out_ref)
    for r in range(PARTS // 4):
        onehot = jnp.concatenate(
            [jnp.where(columns[:, p : p + 1] == lanes, 1.0, 0.0).astype(BF16) for p in range(4 * r, 4 * r + 4)], axis=0
        )
        rows = lax.dot_general(onehot, feats, (((1,), (1,)), ((), ())), preferred_element_type=F32).astype(BF16)
        for p in range(4):
            for h in range(2):
                taken = rows[32 * p + 16 * h : 32 * p + 16 * h + 16]
                out_ref[(4 * r + p) * 16 : (4 * r + p) * 16 + 16, 64 * h : 64 * h + SL] = taken


def build_counts(nbr_ref, deg_ref, cnt_ref, lanes, place, size, field, group):
    rows8 = lax.broadcasted_iota(I32, (8, 128), 0)
    idx = place(nbr_ref[:, lanes])
    valid = (lax.broadcasted_iota(I32, (FAN, 128), 0) < deg_ref[:, lanes]) & (idx >= 0) & (idx < size)
    which = jnp.zeros_like(idx)
    for j in range(1, 6):
        which = which + jnp.where(idx >= j * field, 1, 0)
    q = idx - which * field
    v = jnp.left_shift(jnp.ones_like(idx), which * 5)
    above = jnp.where(valid, lax.shift_right_arithmetic(q, group.bit_length() - 1), -1)
    below = jnp.bitwise_and(q, group - 1)
    aboves, tables = [], []
    for k in range(FAN):
        aboves.append(jnp.broadcast_to(above[k : k + 1], (8, 128)))
        low = jnp.broadcast_to(below[k : k + 1], (8, 128))
        value = jnp.broadcast_to(v[k : k + 1], (8, 128))
        tables.append([jnp.where(low == rows8 + 8 * c, value, 0) for c in range(group // 8)])
    for g in range(field // group):
        accs = [jnp.zeros((8, 128), I32)] * (group // 8)
        for k in range(FAN):
            hit = aboves[k] == g
            accs = [acc + jnp.where(hit, tables[k][c], 0) for c, acc in enumerate(accs)]
        for c in range(0, group // 8, 2):
            both = jnp.concatenate(accs[c : c + 2], axis=0)
            for j in range(6):
                count = jnp.bitwise_and(both, 31 << (5 * j)).astype(F32).astype(BF16)
                row = j * field + g * group + 8 * c
                cnt_ref[row : row + 16, :] = count


def scaled(values, field):
    slot = lax.broadcasted_iota(I32, values.shape, 1)
    scale = jnp.full(values.shape, 2.0**12, F32)
    for j in range(1, 6):
        scale = jnp.where(slot >= j * field, 2.0 ** (12 - 5 * j), scale)
    return (values.astype(F32) * scale).astype(BF16)


def pipelined(nbr_ref, deg_ref, buffers, place, size, field, group, multiply):
    def lanes(n):
        return pl.ds(pl.multiple_of(n * 128, 128), 128)

    def pair(n, carry):
        multiply(jnp.maximum(2 * n - 1, 0), buffers[1])
        build_counts(nbr_ref, deg_ref, buffers[0], lanes(2 * n), place, size, field, group)
        multiply(2 * n, buffers[0])
        build_counts(nbr_ref, deg_ref, buffers[1], lanes(2 * n + 1), place, size, field, group)
        return carry

    lax.fori_loop(0, NB // 2, pair, 0)
    multiply(NB - 1, buffers[1])


def own_kernel(nbr_ref, deg_ref, feat_ref, own_ref, cnt0, cnt1, feats):
    feats[...] = scaled(feat_ref[...], OWN_FIELD)

    def multiply(n, cnt):
        own_ref[n] = jnp.dot(feats[...], cnt[0:NP, :], preferred_element_type=F32)

    pipelined(nbr_ref, deg_ref, (cnt0, cnt1), lambda idx: idx, NP, OWN_FIELD, 32, multiply)


def finish_kernel(recv_ref, nbr_ref, deg_ref, own_ref, feat_ref, out_ref, cnt0, cnt1, recv):
    both = jnp.transpose(recv_ref[...].astype(F32), (1, 0))
    recv[...] = scaled(jnp.concatenate([both[0:SL], both[64 : 64 + SL]], axis=1), FAR_FIELD)

    def place(idx):
        far = idx - NP
        part = jnp.bitwise_and(lax.shift_right_arithmetic(far, 4), 1)
        row = lax.shift_right_arithmetic(far, 5) * 16 + jnp.bitwise_and(far, 15)
        return jnp.where(far < 0, -1, part * (SENT // 2) + row)

    def multiply(n, cnt):
        lanes = pl.ds(pl.multiple_of(n * 128, 128), 128)
        far = jnp.dot(recv[...], cnt[0:SENT, :], preferred_element_type=F32)
        inverse = 1.0 / deg_ref[:, lanes].astype(F32)
        out_ref[n, 0:SL, :] = feat_ref[:, lanes]
        out_ref[n, SL : 2 * SL, :] = ((own_ref[n] + far) * 2.0**-12 * inverse).astype(BF16)

    pipelined(nbr_ref, deg_ref, (cnt0, cnt1), place, SENT, FAR_FIELD, 16, multiply)


def columns(*refs):
    rows = [ref[...] for ref in refs] + [jnp.zeros((8 - len(refs), HID), F32)]
    return jnp.transpose(jnp.concatenate(rows, axis=0), (1, 0))


def preact_kernel(block_ref, ws_ref, wn_ref, bias_ref, as_ref, an_ref, mask_ref, score_ref):
    dims = (((0,), (0,)), ((), ()))
    pre = lax.dot_general(block_ref[:, 0:SL, :].reshape(SL * NB, 128), ws_ref[...], dims, preferred_element_type=F32)
    pre = pre + lax.dot_general(block_ref[:, SL : 2 * SL, :].reshape(SL * NB, 128), wn_ref[...], dims, preferred_element_type=F32)
    par = columns(bias_ref, as_ref, an_ref)
    pre = jnp.transpose(pre, (1, 0)) + par[:, 0:1]
    hidden = jnp.maximum(pre, 0.0)
    mask_ref[...] = jnp.where(pre > 0, 1.0, 0.0).astype(BF16)
    own = jnp.sum(hidden * par[:, 1:2], axis=0, keepdims=True)
    neigh = jnp.sum(hidden * par[:, 2:3], axis=0, keepdims=True)
    both = jnp.concatenate([own, neigh, jnp.zeros((6, 128), F32)], axis=0)
    for b in range(NB):
        score_ref[b] = both


def lane_gather(row, idx):
    return jnp.take_along_axis(jnp.broadcast_to(row, idx.shape), idx, axis=1)


def boundary_score_kernel(score_ref, send_ref, out_ref):
    idx = jnp.concatenate([send_ref[0], jnp.zeros((PARTS, 96), I32)], axis=1)
    low = jnp.bitwise_and(idx, 127)
    high = lax.shift_right_logical(idx, 7)
    acc = jnp.zeros((PARTS, 128), F32)
    for b in range(NB):
        acc = jnp.where(high == b, lane_gather(score_ref[b, 1:2, :], low), acc)
    for p in range(PARTS):
        out_ref[p] = acc[p : p + 1, :]


def own_logit_kernel(score_ref, nbr_ref, deg_ref, out_ref):
    def one(f, carry):
        lanes = pl.ds(pl.multiple_of(f * 128, 128), 128)
        idx = nbr_ref[:, lanes]
        low = jnp.bitwise_and(idx, 127)
        high = lax.shift_right_logical(idx, 7)
        acc = jnp.zeros((FAN, 128), F32)
        for r in range(NB):
            acc = jnp.where(high == r, lane_gather(score_ref[r, 1:2, :], low), acc)
        valid = lax.broadcasted_iota(I32, (FAN, 128), 0) < deg_ref[:, lanes]
        out_ref[:, lanes] = jnp.sum(jnp.where(valid, acc, 0.0), axis=0, keepdims=True)
        return carry

    lax.fori_loop(0, NB, one, 0)


def dense_rows(ref):
    lane = lax.broadcasted_iota(I32, (8, 128), 1)
    acc = jnp.zeros((8, 128), F32)
    for g in range(4):
        rows = jnp.concatenate([ref[4 * r + g] for r in range(8)], axis=0)
        rows = pltpu.roll(rows, 32 * g, 1) if g else rows
        acc = jnp.where(lax.shift_right_logical(lane, 5) == g, rows, acc)
    return acc


def logit_kernel(score_ref, own_ref, far_ref, nbr_ref, deg_ref, label_ref, logit_ref, dlogit_ref, slot_ref, out_ref, table, acc_ref):
    table[...] = dense_rows(far_ref)
    acc_ref[...] = jnp.zeros_like(acc_ref)
    highs = SLOTS // 128
    high_rows = lax.broadcasted_iota(I32, (highs, 128), 0)
    low_rows = lax.broadcasted_iota(I32, (16, 128), 0)
    one16, zero16 = jnp.ones((16, 128), BF16), jnp.zeros((16, 128), BF16)

    def one(f, left, right):
        lanes = pl.ds(pl.multiple_of(f * 128, 128), 128)
        idx = nbr_ref[:, lanes]
        low = jnp.bitwise_and(idx, 127)
        high = lax.shift_right_logical(idx, 7)
        acc = jnp.zeros((FAN, 128), F32)
        for r in range(SENT // 128):
            acc = jnp.where(high == NB + r, lane_gather(table[r : r + 1, :], low), acc)
        degree = deg_ref[:, lanes]
        valid = lax.broadcasted_iota(I32, (FAN, 128), 0) < degree
        inverse = 1.0 / degree.astype(F32)
        total = own_ref[:, lanes] + jnp.sum(jnp.where(valid, acc, 0.0), axis=0, keepdims=True)
        logits = score_ref[f, 0:1, :] + total * inverse
        logit_ref[:, lanes] = logits
        dlogit = (jax.nn.sigmoid(logits) - label_ref[:, lanes].astype(F32)) * (float(NP * PARTS) ** -0.5)
        dlogit_ref[:, lanes] = dlogit
        thirds = [t.astype(F32) for t in split3(dlogit * inverse)]
        high = jnp.where(valid, high, -1)
        for k in range(FAN):
            hit = high[k : k + 1] == high_rows
            left.append(jnp.concatenate([jnp.where(hit, t, 0.0) for t in thirds], axis=0).astype(BF16))
            offset = (jnp.broadcast_to(low[k : k + 1], (16, 128)) - low_rows).astype(F32).astype(BF16)
            right.append(jnp.concatenate([jnp.where(offset == 16.0 * j, one16, zero16) for j in range(8)], axis=0))

    def pair(n, carry):
        left, right = [], []
        one(2 * n, left, right)
        one(2 * n + 1, left, right)
        acc_ref[...] += lax.dot_general(
            jnp.concatenate(left, axis=1),
            jnp.concatenate(right, axis=1),
            (((1,), (1,)), ((), ())),
            preferred_element_type=F32,
        )
        return carry

    lax.fori_loop(0, NB // 2, pair, 0)
    slot = acc_ref[0:highs] + acc_ref[highs : 2 * highs] + acc_ref[2 * highs : 3 * highs]
    slot_ref[...] = slot
    for r in range(8):
        row = slot[NB + r : NB + r + 1, :]
        for g in range(4):
            out_ref[4 * r + g] = pltpu.roll(row, 128 - 32 * g, 1) if g else row


def grad_kernel(ret_ref, send_ref, slot_ref, dlogit_ref, as_ref, an_ref, mask_ref, block_ref, out_ref, dneigh, wide_s, wide_n, acc):
    step = pl.program_id(0)
    per = mask_ref.shape[0]

    @pl.when(step == 0)
    def _():
        send = jnp.transpose(send_ref[0], (1, 0))
        back = jnp.transpose(jnp.concatenate([ret_ref[p] for p in range(PARTS)], axis=0), (1, 0))[0:B]
        lane = lax.broadcasted_iota(I32, (8, 128), 1)
        totals = [jnp.zeros((8, 128), F32) for _ in range(NB)]
        for p in range(PARTS):
            for c in range(B // 8):
                node = jnp.broadcast_to(send[8 * c : 8 * c + 8, p : p + 1], (8, 128)) - lane
                value = jnp.broadcast_to(back[8 * c : 8 * c + 8, p : p + 1], (8, 128))
                for f in range(NB):
                    totals[f] = totals[f] + jnp.where(node == f * 128, value, 0.0)
        for f in range(NB):
            lanes = slice(f * 128, (f + 1) * 128)
            dneigh[:, lanes] = slot_ref[f : f + 1, :] + jnp.sum(totals[f], axis=0, keepdims=True)
        par = columns(as_ref, an_ref)
        wide_s[...] = jnp.broadcast_to(par[:, 0:1], (HID, 128))
        wide_n[...] = jnp.broadcast_to(par[:, 1:2], (HID, 128))
        acc[...] = jnp.zeros_like(acc)

    for b in range(per):
        lanes = pl.ds(pl.multiple_of((step * per + b) * 128, 128), 128)
        grad = wide_s[...] * dlogit_ref[:, lanes] + wide_n[...] * dneigh[:, lanes]
        dpre = grad.astype(BF16) * mask_ref[b]
        acc[...] += lax.dot_general(block_ref[b], dpre, (((1,), (1,)), ((), ())), preferred_element_type=F32)

    @pl.when(step == pl.num_programs(0) - 1)
    def _():
        for tile in range(12):
            for half in range(2):
                for c in range(4):
                    row = tile * 8 + half * 4
                    out_ref[(tile * 2 + half) * 4 + c] = acc[row : row + 4, c * 128 : (c + 1) * 128].astype(BF16)


def sum_kernel(in_ref, out_ref):
    for c in range(3):
        total = in_ref[c].astype(F32)
        for p in range(1, PARTS):
            total = total + in_ref[3 * p + c].astype(F32)
        total = total.astype(BF16)
        for p in range(PARTS):
            out_ref[3 * p + c] = total


def place_kernel(in_ref, self_ref, neigh_ref):
    for tile in range(12):
        for half in range(2):
            for c in range(4):
                value = in_ref[(tile * 2 + half) * 4 + c].astype(F32)
                row = (tile % 6) * 8 + half * 4
                ref = self_ref if tile < 6 else neigh_ref
                ref[row : row + 4, c * 128 : (c + 1) * 128] = value


def whole(shape):
    return pl.BlockSpec(shape, lambda *_: (0,) * len(shape))


def resident():
    return pl.BlockSpec(memory_space=pltpu.VMEM)


def near(x):
    return pltpu.with_memory_space_constraint(x, pltpu.VMEM)


def exchange(x, axis):
    return near(lax.all_to_all(x, axis, split_axis=0, concat_axis=0, tiled=True))


def body(features, neighbors, degree, send_rows, labels, w_self, w_neigh, bias, a_self, a_neigh):
    degree = degree.reshape(1, NP)
    labels = labels.reshape(1, NP)
    bias, a_self, a_neigh = bias.reshape(1, HID), a_self.reshape(1, HID), a_neigh.reshape(1, HID)

    outgoing = call(send_kernel, sds((SENT // 2, 128), BF16), "send")(features, send_rows)
    incoming = exchange(outgoing, "dom")

    own = call(
        own_kernel,
        sds((NB, SL, 128), F32),
        "own",
        scratch_shapes=[pltpu.VMEM((6 * OWN_FIELD, 128), BF16)] * 2 + [pltpu.VMEM((SL, NP), BF16)],
    )(neighbors, degree, features)
    block = call(
        finish_kernel,
        sds((NB, 2 * SL, 128), BF16),
        "finish",
        scratch_shapes=[pltpu.VMEM((6 * FAR_FIELD, 128), BF16)] * 2 + [pltpu.VMEM((SL, SENT), BF16)],
    )(incoming, neighbors, degree, own, features)
    mine = exchange(block, "feat")

    mask, scores = call(preact_kernel, (sds((HID, 128), BF16), sds((NB, 8, 128), F32)), "preact")(
        mine, near(w_self), near(w_neigh), bias, a_self, a_neigh
    )
    scores = exchange(scores, "feat")
    masks = lax.all_gather(mask, "feat", axis=0, tiled=False)
    score_out = call(boundary_score_kernel, sds((PARTS, 1, 128), F32), "bscore")(scores, near(send_rows))
    score_in = exchange(score_out, "dom")
    own_total = call(own_logit_kernel, sds((1, NP), F32), "ownlogit")(scores, neighbors, degree)

    logits, dlogit, slot, slot_out = call(
        logit_kernel,
        (sds((1, NP), F32), sds((1, NP), F32), sds((SLOTS // 128, 128), F32), sds((PARTS, 1, 128), F32)),
        "logit",
        scratch_shapes=[pltpu.VMEM((SENT // 128, 128), F32), pltpu.VMEM((3 * SLOTS // 128, 128), F32)],
    )(scores, own_total, score_in, neighbors, degree, labels)
    returned = exchange(slot_out, "dom")

    per = 4
    partial = call(
        grad_kernel,
        sds((96, 4, 128), BF16),
        "grad",
        grid=(NB // per,),
        in_specs=[
            resident(),
            whole((1, B, PARTS)),
            whole((SLOTS // 128, 128)),
            whole((1, NP)),
            whole((1, HID)),
            whole((1, HID)),
            pl.BlockSpec((per, HID, 128), lambda i: (i, 0, 0)),
            pl.BlockSpec((per, 2 * SL, 128), lambda i: (i, 0, 0)),
        ],
        out_specs=whole((96, 4, 128)),
        scratch_shapes=[
            pltpu.VMEM((1, NP), F32),
            pltpu.VMEM((HID, 128), F32),
            pltpu.VMEM((HID, 128), F32),
            pltpu.VMEM((2 * SL, HID), F32),
        ],
    )(returned, send_rows, slot, dlogit, a_self, a_neigh, masks, block)
    shares = exchange(partial, "dom")
    summed = call(sum_kernel, sds((96, 4, 128), BF16), "sum")(shares)
    summed = exchange(summed, "dom")
    grad_self, grad_neigh = call(place_kernel, (sds((SL, HID), F32), sds((SL, HID), F32)), "place")(summed)
    return (logits.reshape(NP), grad_self, grad_neigh)


def solution(mesh):
    return jax.shard_map(
        body,
        mesh=mesh,
        in_specs=(
            P("feat", "dom"),
            P(None, "dom"),
            P("dom"),
            P("dom", None, None),
            P("dom"),
            P(),
            P(),
            P(),
            P(),
            P(),
        ),
        out_specs=(P("dom"), P("feat", None), P("feat", None)),
        check_vma=False,
    )
```

```python
import jax
import jax.numpy as jnp
from jax import lax
from jax.experimental import pallas as pl
from jax.experimental.pallas import tpu as pltpu
from jax.sharding import PartitionSpec as P

F32 = jnp.float32
BF16 = jnp.bfloat16
I32 = jnp.int32

SL = 48
NP = 2048
NB = 16
PARTS = 32
B = 32
SENT = 1024
SLOTS = 3072
FAN = 16
HID = 512
OWN_FIELD = 352
FAR_FIELD = 176


def call(kernel, out_shape, name, **kw):
    return pl.pallas_call(kernel, out_shape=out_shape, name=name, **kw)


def sds(shape, dtype):
    return jax.ShapeDtypeStruct(shape, dtype)


def split3(x):
    hi = x.astype(BF16)
    rest = x - hi.astype(F32)
    mid = rest.astype(BF16)
    low = (rest - mid.astype(F32)).astype(BF16)
    return hi, mid, low


def send_kernel(feat_ref, send_ref, out_ref):
    feats = feat_ref[...]
    columns = jnp.transpose(send_ref[0], (1, 0))
    lanes = lax.broadcasted_iota(I32, (B, NP), 1)
    out_ref[...] = jnp.zeros_like(out_ref)
    for r in range(PARTS // 4):
        onehot = jnp.concatenate(
            [jnp.where(columns[:, p : p + 1] == lanes, 1.0, 0.0).astype(BF16) for p in range(4 * r, 4 * r + 4)], axis=0
        )
        rows = lax.dot_general(onehot, feats, (((1,), (1,)), ((), ())), preferred_element_type=F32).astype(BF16)
        for p in range(4):
            for h in range(2):
                taken = rows[32 * p + 16 * h : 32 * p + 16 * h + 16]
                out_ref[(4 * r + p) * 16 : (4 * r + p) * 16 + 16, 64 * h : 64 * h + SL] = taken


def build_counts(nbr_ref, deg_ref, cnt_ref, lanes, place, size, field, group):
    rows8 = lax.broadcasted_iota(I32, (8, 128), 0)
    idx = place(nbr_ref[:, lanes])
    valid = (lax.broadcasted_iota(I32, (FAN, 128), 0) < deg_ref[:, lanes]) & (idx >= 0) & (idx < size)
    which = jnp.zeros_like(idx)
    for j in range(1, 6):
        which = which + jnp.where(idx >= j * field, 1, 0)
    q = idx - which * field
    v = jnp.left_shift(jnp.ones_like(idx), which * 5)
    above = jnp.where(valid, lax.shift_right_arithmetic(q, group.bit_length() - 1), -1)
    below = jnp.bitwise_and(q, group - 1)
    aboves, tables = [], []
    for k in range(FAN):
        aboves.append(jnp.broadcast_to(above[k : k + 1], (8, 128)))
        low = jnp.broadcast_to(below[k : k + 1], (8, 128))
        value = jnp.broadcast_to(v[k : k + 1], (8, 128))
        tables.append([jnp.where(low == rows8 + 8 * c, value, 0) for c in range(group // 8)])
    for g in range(field // group):
        accs = [jnp.zeros((8, 128), I32)] * (group // 8)
        for k in range(FAN):
            hit = aboves[k] == g
            accs = [acc + jnp.where(hit, tables[k][c], 0) for c, acc in enumerate(accs)]
        for c in range(0, group // 8, 2):
            both = jnp.concatenate(accs[c : c + 2], axis=0)
            for j in range(6):
                count = jnp.bitwise_and(both, 31 << (5 * j)).astype(F32).astype(BF16)
                row = j * field + g * group + 8 * c
                cnt_ref[row : row + 16, :] = count


def scaled(values, field):
    slot = lax.broadcasted_iota(I32, values.shape, 1)
    scale = jnp.full(values.shape, 2.0**12, F32)
    for j in range(1, 6):
        scale = jnp.where(slot >= j * field, 2.0 ** (12 - 5 * j), scale)
    return (values.astype(F32) * scale).astype(BF16)


def pipelined(nbr_ref, deg_ref, buffers, place, size, field, group, multiply):
    def lanes(n):
        return pl.ds(pl.multiple_of(n * 128, 128), 128)

    def pair(n, carry):
        multiply(jnp.maximum(2 * n - 1, 0), buffers[1])
        build_counts(nbr_ref, deg_ref, buffers[0], lanes(2 * n), place, size, field, group)
        multiply(2 * n, buffers[0])
        build_counts(nbr_ref, deg_ref, buffers[1], lanes(2 * n + 1), place, size, field, group)
        return carry

    blocks = deg_ref.shape[1] // 128
    lax.fori_loop(0, blocks // 2, pair, 0)
    multiply(blocks - 1, buffers[1])


def own_kernel(nbr_ref, deg_ref, feat_ref, own_ref, cnt0, cnt1, feats):
    @pl.when(pl.program_id(0) == 0)
    def _():
        feats[...] = scaled(feat_ref[...], OWN_FIELD)

    def multiply(n, cnt):
        own_ref[n] = jnp.dot(feats[...], cnt[0:NP, :], preferred_element_type=F32)

    pipelined(nbr_ref, deg_ref, (cnt0, cnt1), lambda idx: idx, NP, OWN_FIELD, 32, multiply)


def finish_kernel(recv_ref, nbr_ref, deg_ref, own_ref, feat_ref, out_ref, cnt0, cnt1, recv):
    @pl.when(pl.program_id(0) == 0)
    def _():
        both = jnp.transpose(recv_ref[...].astype(F32), (1, 0))
        recv[...] = scaled(jnp.concatenate([both[0:SL], both[64 : 64 + SL]], axis=1), FAR_FIELD)

    def place(idx):
        far = idx - NP
        part = jnp.bitwise_and(lax.shift_right_arithmetic(far, 4), 1)
        row = lax.shift_right_arithmetic(far, 5) * 16 + jnp.bitwise_and(far, 15)
        return jnp.where(far < 0, -1, part * (SENT // 2) + row)

    def multiply(n, cnt):
        lanes = pl.ds(pl.multiple_of(n * 128, 128), 128)
        far = jnp.dot(recv[...], cnt[0:SENT, :], preferred_element_type=F32)
        inverse = 1.0 / deg_ref[:, lanes].astype(F32)
        out_ref[n, 0:SL, :] = feat_ref[:, lanes]
        out_ref[n, SL : 2 * SL, :] = ((own_ref[n] + far) * 2.0**-12 * inverse).astype(BF16)

    pipelined(nbr_ref, deg_ref, (cnt0, cnt1), place, SENT, FAR_FIELD, 16, multiply)


def columns(*refs):
    rows = [ref[...] for ref in refs] + [jnp.zeros((8 - len(refs), HID), F32)]
    return jnp.transpose(jnp.concatenate(rows, axis=0), (1, 0))


def preact_kernel(block_ref, ws_ref, wn_ref, bias_ref, as_ref, an_ref, mask_ref, score_ref):
    dims = (((0,), (0,)), ((), ()))
    pre = lax.dot_general(block_ref[:, 0:SL, :].reshape(SL * NB, 128), ws_ref[...], dims, preferred_element_type=F32)
    pre = pre + lax.dot_general(block_ref[:, SL : 2 * SL, :].reshape(SL * NB, 128), wn_ref[...], dims, preferred_element_type=F32)
    par = columns(bias_ref, as_ref, an_ref)
    pre = jnp.transpose(pre, (1, 0)) + par[:, 0:1]
    hidden = jnp.maximum(pre, 0.0)
    mask_ref[...] = jnp.where(pre > 0, 1.0, 0.0).astype(BF16)
    own = jnp.sum(hidden * par[:, 1:2], axis=0, keepdims=True)
    neigh = jnp.sum(hidden * par[:, 2:3], axis=0, keepdims=True)
    both = jnp.concatenate([own, neigh, jnp.zeros((6, 128), F32)], axis=0)
    for b in range(NB):
        score_ref[b] = both


def lane_gather(row, idx):
    return jnp.take_along_axis(jnp.broadcast_to(row, idx.shape), idx, axis=1)


def boundary_score_kernel(score_ref, send_ref, out_ref):
    idx = jnp.concatenate([send_ref[0], jnp.zeros((PARTS, 96), I32)], axis=1)
    low = jnp.bitwise_and(idx, 127)
    high = lax.shift_right_logical(idx, 7)
    acc = jnp.zeros((PARTS, 128), F32)
    for b in range(NB):
        acc = jnp.where(high == b, lane_gather(score_ref[b, 1:2, :], low), acc)
    for p in range(PARTS):
        out_ref[p] = acc[p : p + 1, :]


def own_logit_kernel(score_ref, nbr_ref, deg_ref, out_ref):
    def one(f, carry):
        lanes = pl.ds(pl.multiple_of(f * 128, 128), 128)
        idx = nbr_ref[:, lanes]
        low = jnp.bitwise_and(idx, 127)
        high = lax.shift_right_logical(idx, 7)
        acc = jnp.zeros((FAN, 128), F32)
        for r in range(NB):
            acc = jnp.where(high == r, lane_gather(score_ref[r, 1:2, :], low), acc)
        valid = lax.broadcasted_iota(I32, (FAN, 128), 0) < deg_ref[:, lanes]
        out_ref[:, lanes] = jnp.sum(jnp.where(valid, acc, 0.0), axis=0, keepdims=True)
        return carry

    lax.fori_loop(0, NB, one, 0)


def dense_rows(parts, dtype=F32):
    lane = lax.broadcasted_iota(I32, (8, 128), 1)
    acc = jnp.zeros((8, 128), dtype)
    for g in range(4):
        rows = jnp.concatenate([parts[4 * r + g] for r in range(8)], axis=0)
        rows = pltpu.roll(rows, 32 * g, 1) if g else rows
        acc = jnp.where(lax.shift_right_logical(lane, 5) == g, rows, acc)
    return acc


def logit_kernel(score_ref, own_ref, far_ref, nbr_ref, deg_ref, label_ref, logit_ref, dlogit_ref, slot_ref, out_ref, table, acc_ref):
    table[...] = dense_rows(far_ref)
    acc_ref[...] = jnp.zeros_like(acc_ref)
    highs = SLOTS // 128
    high_rows = lax.broadcasted_iota(I32, (highs, 128), 0)
    low_rows = lax.broadcasted_iota(I32, (16, 128), 0)
    one16, zero16 = jnp.ones((16, 128), BF16), jnp.zeros((16, 128), BF16)

    def one(f, left, right):
        lanes = pl.ds(pl.multiple_of(f * 128, 128), 128)
        idx = nbr_ref[:, lanes]
        low = jnp.bitwise_and(idx, 127)
        high = lax.shift_right_logical(idx, 7)
        acc = jnp.zeros((FAN, 128), F32)
        for r in range(SENT // 128):
            acc = jnp.where(high == NB + r, lane_gather(table[r : r + 1, :], low), acc)
        degree = deg_ref[:, lanes]
        valid = lax.broadcasted_iota(I32, (FAN, 128), 0) < degree
        inverse = 1.0 / degree.astype(F32)
        total = own_ref[:, lanes] + jnp.sum(jnp.where(valid, acc, 0.0), axis=0, keepdims=True)
        logits = score_ref[f, 0:1, :] + total * inverse
        logit_ref[:, lanes] = logits
        dlogit = (jax.nn.sigmoid(logits) - label_ref[:, lanes].astype(F32)) * (float(NP * PARTS) ** -0.5)
        dlogit_ref[:, lanes] = dlogit
        thirds = [t.astype(F32) for t in split3(dlogit * inverse)]
        high = jnp.where(valid, high, -1)
        for k in range(FAN):
            hit = high[k : k + 1] == high_rows
            left.append(jnp.concatenate([jnp.where(hit, t, 0.0) for t in thirds], axis=0).astype(BF16))
            offset = (jnp.broadcast_to(low[k : k + 1], (16, 128)) - low_rows).astype(F32).astype(BF16)
            right.append(jnp.concatenate([jnp.where(offset == 16.0 * j, one16, zero16) for j in range(8)], axis=0))

    def several(n, carry):
        left, right = [], []
        for u in range(4):
            one(4 * n + u, left, right)
        acc_ref[...] += lax.dot_general(
            jnp.concatenate(left, axis=1),
            jnp.concatenate(right, axis=1),
            (((1,), (1,)), ((), ())),
            preferred_element_type=F32,
        )
        return carry

    lax.fori_loop(0, NB // 4, several, 0)
    slot = acc_ref[0:highs] + acc_ref[highs : 2 * highs] + acc_ref[2 * highs : 3 * highs]
    slot_ref[...] = slot
    for r in range(8):
        row = slot[NB + r : NB + r + 1, :]
        for g in range(4):
            out_ref[4 * r + g] = pltpu.roll(row, 128 - 32 * g, 1) if g else row


def grad_kernel(ret_ref, send_ref, slot_ref, dlogit_ref, as_ref, an_ref, mask_ref, block_ref, out_ref, dneigh, wide_s, wide_n, acc):
    step = pl.program_id(0)
    per = mask_ref.shape[0]

    @pl.when(step == 0)
    def _():
        send = jnp.concatenate([send_ref[0], jnp.zeros((PARTS, 96), I32)], axis=1)
        send = dense_rows([send[p : p + 1] for p in range(PARTS)], I32)
        thirds = [t.astype(F32) for t in split3(dense_rows(ret_ref))]
        low = jnp.bitwise_and(send, 127)
        high = lax.shift_right_logical(send, 7)
        high_rows = lax.broadcasted_iota(I32, (NB, 128), 0)
        low_rows = lax.broadcasted_iota(I32, (128, 128), 0)
        left, right = [], []
        for r in range(SENT // 128):
            hit = high[r : r + 1] == high_rows
            left.append(jnp.concatenate([jnp.where(hit, t[r : r + 1], 0.0) for t in thirds], axis=0).astype(BF16))
            right.append(jnp.where(low[r : r + 1] == low_rows, 1.0, 0.0).astype(BF16))
        sums = lax.dot_general(
            jnp.concatenate(left, axis=1),
            jnp.concatenate(right, axis=1),
            (((1,), (1,)), ((), ())),
            preferred_element_type=F32,
        )
        sums = slot_ref[0:NB] + (sums[0:NB] + sums[NB : 2 * NB] + sums[2 * NB : 3 * NB])
        for f in range(NB):
            dneigh[:, f * 128 : (f + 1) * 128] = sums[f : f + 1]
        par = columns(as_ref, an_ref)
        wide_s[...] = jnp.broadcast_to(par[:, 0:1], (HID, 128))
        wide_n[...] = jnp.broadcast_to(par[:, 1:2], (HID, 128))
        acc[...] = jnp.zeros_like(acc)

    for b in range(per):
        lanes = pl.ds(pl.multiple_of((step * per + b) * 128, 128), 128)
        grad = wide_s[...] * dlogit_ref[:, lanes] + wide_n[...] * dneigh[:, lanes]
        dpre = grad.astype(BF16) * mask_ref[b]
        acc[...] += lax.dot_general(block_ref[b], dpre, (((1,), (1,)), ((), ())), preferred_element_type=F32)

    @pl.when(step == pl.num_programs(0) - 1)
    def _():
        for tile in range(12):
            for half in range(2):
                for c in range(4):
                    row = tile * 8 + half * 4
                    out_ref[(tile * 2 + half) * 4 + c] = acc[row : row + 4, c * 128 : (c + 1) * 128].astype(BF16)


def sum_kernel(in_ref, out_ref):
    for c in range(3):
        total = in_ref[c].astype(F32)
        for p in range(1, PARTS):
            total = total + in_ref[3 * p + c].astype(F32)
        total = total.astype(BF16)
        for p in range(PARTS):
            out_ref[3 * p + c] = total


def place_kernel(in_ref, self_ref, neigh_ref):
    for tile in range(12):
        for half in range(2):
            for c in range(4):
                value = in_ref[(tile * 2 + half) * 4 + c].astype(F32)
                row = (tile % 6) * 8 + half * 4
                ref = self_ref if tile < 6 else neigh_ref
                ref[row : row + 4, c * 128 : (c + 1) * 128] = value


def whole(shape):
    return pl.BlockSpec(shape, lambda *_: (0,) * len(shape))


def resident():
    return pl.BlockSpec(memory_space=pltpu.VMEM)


def near(x):
    return pltpu.with_memory_space_constraint(x, pltpu.VMEM)


def exchange(x, axis):
    return near(lax.all_to_all(x, axis, split_axis=0, concat_axis=0, tiled=True))


def body(features, neighbors, degree, send_rows, labels, w_self, w_neigh, bias, a_self, a_neigh):
    degree = degree.reshape(1, NP)
    labels = labels.reshape(1, NP)
    bias, a_self, a_neigh = bias.reshape(1, HID), a_self.reshape(1, HID), a_neigh.reshape(1, HID)

    outgoing = call(send_kernel, sds((SENT // 2, 128), BF16), "send")(features, send_rows)
    incoming = exchange(outgoing, "dom")

    steps = 2
    nbr_spec = pl.BlockSpec((FAN, NP // steps), lambda i: (0, i))
    deg_spec = pl.BlockSpec((1, NP // steps), lambda i: (0, i))
    col_spec = pl.BlockSpec((SL, NP // steps), lambda i: (0, i))
    own_spec = pl.BlockSpec((NB // steps, SL, 128), lambda i: (i, 0, 0))
    own = call(
        own_kernel,
        sds((NB, SL, 128), F32),
        "own",
        grid=(steps,),
        in_specs=[nbr_spec, deg_spec, whole((SL, NP))],
        out_specs=own_spec,
        scratch_shapes=[pltpu.VMEM((6 * OWN_FIELD, 128), BF16)] * 2 + [pltpu.VMEM((SL, NP), BF16)],
    )(neighbors, degree, features)
    block = call(
        finish_kernel,
        sds((NB, 2 * SL, 128), BF16),
        "finish",
        grid=(steps,),
        in_specs=[resident(), nbr_spec, deg_spec, own_spec, col_spec],
        out_specs=pl.BlockSpec((NB // steps, 2 * SL, 128), lambda i: (i, 0, 0)),
        scratch_shapes=[pltpu.VMEM((6 * FAR_FIELD, 128), BF16)] * 2 + [pltpu.VMEM((SL, SENT), BF16)],
    )(incoming, neighbors, degree, own, features)
    mine = exchange(block, "feat")

    mask, scores = call(preact_kernel, (sds((HID, 128), BF16), sds((NB, 8, 128), F32)), "preact")(
        mine, near(w_self), near(w_neigh), bias, a_self, a_neigh
    )
    scores = exchange(scores, "feat")
    masks = lax.all_gather(mask, "feat", axis=0, tiled=False)
    score_out = call(boundary_score_kernel, sds((PARTS, 1, 128), F32), "bscore")(scores, near(send_rows))
    score_in = exchange(score_out, "dom")
    own_total = call(own_logit_kernel, sds((1, NP), F32), "ownlogit")(scores, neighbors, degree)

    logits, dlogit, slot, slot_out = call(
        logit_kernel,
        (sds((1, NP), F32), sds((1, NP), F32), sds((SLOTS // 128, 128), F32), sds((PARTS, 1, 128), F32)),
        "logit",
        scratch_shapes=[pltpu.VMEM((SENT // 128, 128), F32), pltpu.VMEM((3 * SLOTS // 128, 128), F32)],
    )(scores, own_total, score_in, neighbors, degree, labels)
    returned = exchange(slot_out, "dom")

    per = 4
    partial = call(
        grad_kernel,
        sds((96, 4, 128), BF16),
        "grad",
        grid=(NB // per,),
        in_specs=[
            resident(),
            whole((1, B, PARTS)),
            whole((SLOTS // 128, 128)),
            whole((1, NP)),
            whole((1, HID)),
            whole((1, HID)),
            pl.BlockSpec((per, HID, 128), lambda i: (i, 0, 0)),
            pl.BlockSpec((per, 2 * SL, 128), lambda i: (i, 0, 0)),
        ],
        out_specs=whole((96, 4, 128)),
        scratch_shapes=[
            pltpu.VMEM((1, NP), F32),
            pltpu.VMEM((HID, 128), F32),
            pltpu.VMEM((HID, 128), F32),
            pltpu.VMEM((2 * SL, HID), F32),
        ],
    )(returned, send_rows, slot, dlogit, a_self, a_neigh, masks, block)
    shares = exchange(partial, "dom")
    summed = call(sum_kernel, sds((96, 4, 128), BF16), "sum")(shares)
    summed = exchange(summed, "dom")
    grad_self, grad_neigh = call(place_kernel, (sds((SL, HID), F32), sds((SL, HID), F32)), "place")(summed)
    return (logits.reshape(NP), grad_self, grad_neigh)


def solution(mesh):
    return jax.shard_map(
        body,
        mesh=mesh,
        in_specs=(
            P("feat", "dom"),
            P(None, "dom"),
            P("dom"),
            P("dom", None, None),
            P("dom"),
            P(),
            P(),
            P(),
            P(),
            P(),
        ),
        out_specs=(P("dom"), P("feat", None), P("feat", None)),
        check_vma=False,
    )
```

```python
import jax
import jax.numpy as jnp
from jax import lax
from jax.experimental import pallas as pl
from jax.experimental.pallas import tpu as pltpu
from jax.sharding import PartitionSpec as P

F32 = jnp.float32
BF16 = jnp.bfloat16
I32 = jnp.int32

SL = 48
NP = 2048
NB = 16
PARTS = 32
B = 32
SENT = 1024
SLOTS = 3072
FAN = 16
HID = 512
OWN_FIELD = 352
FAR_FIELD = 176


def call(kernel, out_shape, name, **kw):
    return pl.pallas_call(kernel, out_shape=out_shape, name=name, **kw)


def sds(shape, dtype):
    return jax.ShapeDtypeStruct(shape, dtype)


def split3(x):
    hi = x.astype(BF16)
    rest = x - hi.astype(F32)
    mid = rest.astype(BF16)
    low = (rest - mid.astype(F32)).astype(BF16)
    return hi, mid, low


def send_kernel(feat_ref, send_ref, out_ref):
    feats = feat_ref[...]
    columns = jnp.transpose(send_ref[0], (1, 0))
    lanes = lax.broadcasted_iota(I32, (B, NP), 1)
    out_ref[...] = jnp.zeros_like(out_ref)
    for r in range(PARTS // 4):
        onehot = jnp.concatenate(
            [jnp.where(columns[:, p : p + 1] == lanes, 1.0, 0.0).astype(BF16) for p in range(4 * r, 4 * r + 4)], axis=0
        )
        rows = lax.dot_general(onehot, feats, (((1,), (1,)), ((), ())), preferred_element_type=F32).astype(BF16)
        for p in range(4):
            for h in range(2):
                taken = rows[32 * p + 16 * h : 32 * p + 16 * h + 16]
                out_ref[(4 * r + p) * 16 : (4 * r + p) * 16 + 16, 64 * h : 64 * h + SL] = taken


def build_counts(nbr_ref, deg_ref, cnt_ref, lanes, place, size, field, group):
    rows8 = lax.broadcasted_iota(I32, (8, 128), 0)
    idx = place(nbr_ref[:, lanes])
    valid = (lax.broadcasted_iota(I32, (FAN, 128), 0) < deg_ref[:, lanes]) & (idx >= 0) & (idx < size)
    which = jnp.zeros_like(idx)
    for j in range(1, 6):
        which = which + jnp.where(idx >= j * field, 1, 0)
    q = idx - which * field
    v = jnp.left_shift(jnp.ones_like(idx), which * 5)
    above = jnp.where(valid, lax.shift_right_arithmetic(q, group.bit_length() - 1), -1)
    below = jnp.bitwise_and(q, group - 1)
    aboves, tables = [], []
    for k in range(FAN):
        aboves.append(jnp.broadcast_to(above[k : k + 1], (8, 128)))
        low = jnp.broadcast_to(below[k : k + 1], (8, 128))
        value = jnp.broadcast_to(v[k : k + 1], (8, 128))
        tables.append([jnp.where(low == rows8 + 8 * c, value, 0) for c in range(group // 8)])
    for g in range(field // group):
        accs = [jnp.zeros((8, 128), I32)] * (group // 8)
        for k in range(FAN):
            hit = aboves[k] == g
            accs = [acc + jnp.where(hit, tables[k][c], 0) for c, acc in enumerate(accs)]
        for c in range(0, group // 8, 2):
            both = jnp.concatenate(accs[c : c + 2], axis=0)
            for j in range(6):
                count = jnp.bitwise_and(both, 31 << (5 * j)).astype(F32).astype(BF16)
                row = j * field + g * group + 8 * c
                cnt_ref[row : row + 16, :] = count


def scaled(values, field):
    slot = lax.broadcasted_iota(I32, values.shape, 1)
    scale = jnp.full(values.shape, 2.0**12, F32)
    for j in range(1, 6):
        scale = jnp.where(slot >= j * field, 2.0 ** (12 - 5 * j), scale)
    return (values.astype(F32) * scale).astype(BF16)


def pipelined(nbr_ref, deg_ref, buffers, place, size, field, group, multiply):
    def lanes(n):
        return pl.ds(pl.multiple_of(n * 128, 128), 128)

    def pair(n, carry):
        multiply(jnp.maximum(2 * n - 1, 0), buffers[1])
        build_counts(nbr_ref, deg_ref, buffers[0], lanes(2 * n), place, size, field, group)
        multiply(2 * n, buffers[0])
        build_counts(nbr_ref, deg_ref, buffers[1], lanes(2 * n + 1), place, size, field, group)
        return carry

    blocks = deg_ref.shape[1] // 128
    lax.fori_loop(0, blocks // 2, pair, 0)
    multiply(blocks - 1, buffers[1])


def own_kernel(nbr_ref, deg_ref, feat_ref, own_ref, cnt0, cnt1, feats):
    @pl.when(pl.program_id(0) == 0)
    def _():
        feats[...] = scaled(feat_ref[...], OWN_FIELD)

    def multiply(n, cnt):
        own_ref[n] = jnp.dot(feats[...], cnt[0:NP, :], preferred_element_type=F32)

    pipelined(nbr_ref, deg_ref, (cnt0, cnt1), lambda idx: idx, NP, OWN_FIELD, 32, multiply)


def finish_kernel(recv_ref, nbr_ref, deg_ref, own_ref, feat_ref, out_ref, cnt0, cnt1, recv):
    @pl.when(pl.program_id(0) == 0)
    def _():
        both = jnp.transpose(recv_ref[...].astype(F32), (1, 0))
        recv[...] = scaled(jnp.concatenate([both[0:SL], both[64 : 64 + SL]], axis=1), FAR_FIELD)

    def place(idx):
        far = idx - NP
        part = jnp.bitwise_and(lax.shift_right_arithmetic(far, 4), 1)
        row = lax.shift_right_arithmetic(far, 5) * 16 + jnp.bitwise_and(far, 15)
        return jnp.where(far < 0, -1, part * (SENT // 2) + row)

    def multiply(n, cnt):
        lanes = pl.ds(pl.multiple_of(n * 128, 128), 128)
        far = jnp.dot(recv[...], cnt[0:SENT, :], preferred_element_type=F32)
        inverse = 1.0 / deg_ref[:, lanes].astype(F32)
        out_ref[n, 0:SL, :] = feat_ref[:, lanes]
        out_ref[n, SL : 2 * SL, :] = ((own_ref[n] + far) * 2.0**-12 * inverse).astype(BF16)

    pipelined(nbr_ref, deg_ref, (cnt0, cnt1), place, SENT, FAR_FIELD, 16, multiply)


def columns(*refs):
    rows = [ref[...] for ref in refs] + [jnp.zeros((8 - len(refs), HID), F32)]
    return jnp.transpose(jnp.concatenate(rows, axis=0), (1, 0))


def preact_kernel(block_ref, ws_ref, wn_ref, bias_ref, as_ref, an_ref, mask_ref, score_ref):
    dims = (((0,), (0,)), ((), ()))
    pre = lax.dot_general(block_ref[:, 0:SL, :].reshape(SL * NB, 128), ws_ref[...], dims, preferred_element_type=F32)
    pre = pre + lax.dot_general(block_ref[:, SL : 2 * SL, :].reshape(SL * NB, 128), wn_ref[...], dims, preferred_element_type=F32)
    par = columns(bias_ref, as_ref, an_ref)
    pre = jnp.transpose(pre, (1, 0)) + par[:, 0:1]
    hidden = jnp.maximum(pre, 0.0)
    mask_ref[...] = jnp.where(pre > 0, 1.0, 0.0).astype(BF16)
    own = jnp.sum(hidden * par[:, 1:2], axis=0, keepdims=True)
    neigh = jnp.sum(hidden * par[:, 2:3], axis=0, keepdims=True)
    both = jnp.concatenate([own, neigh, jnp.zeros((6, 128), F32)], axis=0)
    for b in range(NB):
        score_ref[b] = both


def lane_gather(row, idx):
    return jnp.take_along_axis(jnp.broadcast_to(row, idx.shape), idx, axis=1)


def boundary_score_kernel(score_ref, send_ref, out_ref):
    idx = jnp.concatenate([send_ref[0], jnp.zeros((PARTS, 96), I32)], axis=1)
    low = jnp.bitwise_and(idx, 127)
    high = lax.shift_right_logical(idx, 7)
    acc = jnp.zeros((PARTS, 128), F32)
    for b in range(NB):
        acc = jnp.where(high == b, lane_gather(score_ref[b, 1:2, :], low), acc)
    for p in range(PARTS):
        out_ref[p] = acc[p : p + 1, :]


def dense_rows(parts, dtype=F32):
    lane = lax.broadcasted_iota(I32, (8, 128), 1)
    acc = jnp.zeros((8, 128), dtype)
    for g in range(4):
        rows = jnp.concatenate([parts[4 * r + g] for r in range(8)], axis=0)
        rows = pltpu.roll(rows, 32 * g, 1) if g else rows
        acc = jnp.where(lax.shift_right_logical(lane, 5) == g, rows, acc)
    return acc


def logit_kernel(score_ref, far_ref, nbr_ref, deg_ref, label_ref, logit_ref, dlogit_ref, slot_ref, out_ref, table, acc_ref):
    for b in range(NB):
        table[b : b + 1, :] = score_ref[b, 1:2, :]
    table[NB:, :] = dense_rows(far_ref)
    acc_ref[...] = jnp.zeros_like(acc_ref)
    highs = SLOTS // 128
    high_rows = lax.broadcasted_iota(I32, (highs, 128), 0)
    low_rows = lax.broadcasted_iota(I32, (16, 128), 0)
    one16, zero16 = jnp.ones((16, 128), BF16), jnp.zeros((16, 128), BF16)

    def one(f, left, right):
        lanes = pl.ds(pl.multiple_of(f * 128, 128), 128)
        idx = nbr_ref[:, lanes]
        low = jnp.bitwise_and(idx, 127)
        high = lax.shift_right_logical(idx, 7)
        acc = jnp.zeros((FAN, 128), F32)
        for r in range(SLOTS // 128):
            acc = jnp.where(high == r, lane_gather(table[r : r + 1, :], low), acc)
        degree = deg_ref[:, lanes]
        valid = lax.broadcasted_iota(I32, (FAN, 128), 0) < degree
        inverse = 1.0 / degree.astype(F32)
        total = jnp.sum(jnp.where(valid, acc, 0.0), axis=0, keepdims=True)
        logits = score_ref[f, 0:1, :] + total * inverse
        logit_ref[:, lanes] = logits
        dlogit = (jax.nn.sigmoid(logits) - label_ref[:, lanes].astype(F32)) * (float(NP * PARTS) ** -0.5)
        dlogit_ref[:, lanes] = dlogit
        thirds = [t.astype(F32) for t in split3(dlogit * inverse)]
        high = jnp.where(valid, high, -1)
        for k in range(FAN):
            hit = high[k : k + 1] == high_rows
            left.append(jnp.concatenate([jnp.where(hit, t, 0.0) for t in thirds], axis=0).astype(BF16))
            offset = (jnp.broadcast_to(low[k : k + 1], (16, 128)) - low_rows).astype(F32).astype(BF16)
            right.append(jnp.concatenate([jnp.where(offset == 16.0 * j, one16, zero16) for j in range(8)], axis=0))

    def several(n, carry):
        left, right = [], []
        for u in range(4):
            one(4 * n + u, left, right)
        acc_ref[...] += lax.dot_general(
            jnp.concatenate(left, axis=1),
            jnp.concatenate(right, axis=1),
            (((1,), (1,)), ((), ())),
            preferred_element_type=F32,
        )
        return carry

    lax.fori_loop(0, NB // 4, several, 0)
    slot = acc_ref[0:highs] + acc_ref[highs : 2 * highs] + acc_ref[2 * highs : 3 * highs]
    slot_ref[...] = slot
    for r in range(8):
        row = slot[NB + r : NB + r + 1, :]
        for g in range(4):
            out_ref[4 * r + g] = pltpu.roll(row, 128 - 32 * g, 1) if g else row


def grad_kernel(ret_ref, send_ref, slot_ref, dlogit_ref, as_ref, an_ref, mask_ref, block_ref, out_ref, dneigh, wide_s, wide_n, acc):
    step = pl.program_id(0)
    per = mask_ref.shape[0]

    @pl.when(step == 0)
    def _():
        send = jnp.concatenate([send_ref[0], jnp.zeros((PARTS, 96), I32)], axis=1)
        send = dense_rows([send[p : p + 1] for p in range(PARTS)], I32)
        thirds = [t.astype(F32) for t in split3(dense_rows(ret_ref))]
        low = jnp.bitwise_and(send, 127)
        high = lax.shift_right_logical(send, 7)
        high_rows = lax.broadcasted_iota(I32, (NB, 128), 0)
        low_rows = lax.broadcasted_iota(I32, (128, 128), 0)
        left, right = [], []
        for r in range(SENT // 128):
            hit = high[r : r + 1] == high_rows
            left.append(jnp.concatenate([jnp.where(hit, t[r : r + 1], 0.0) for t in thirds], axis=0).astype(BF16))
            right.append(jnp.where(low[r : r + 1] == low_rows, 1.0, 0.0).astype(BF16))
        sums = lax.dot_general(
            jnp.concatenate(left, axis=1),
            jnp.concatenate(right, axis=1),
            (((1,), (1,)), ((), ())),
            preferred_element_type=F32,
        )
        sums = slot_ref[0:NB] + (sums[0:NB] + sums[NB : 2 * NB] + sums[2 * NB : 3 * NB])
        for f in range(NB):
            dneigh[:, f * 128 : (f + 1) * 128] = sums[f : f + 1]
        par = columns(as_ref, an_ref)
        wide_s[...] = jnp.broadcast_to(par[:, 0:1], (HID, 128))
        wide_n[...] = jnp.broadcast_to(par[:, 1:2], (HID, 128))
        acc[...] = jnp.zeros_like(acc)

    for b in range(per):
        lanes = pl.ds(pl.multiple_of((step * per + b) * 128, 128), 128)
        grad = wide_s[...] * dlogit_ref[:, lanes] + wide_n[...] * dneigh[:, lanes]
        dpre = grad.astype(BF16) * mask_ref[b]
        acc[...] += lax.dot_general(block_ref[b], dpre, (((1,), (1,)), ((), ())), preferred_element_type=F32)

    @pl.when(step == pl.num_programs(0) - 1)
    def _():
        for tile in range(12):
            for half in range(2):
                for c in range(4):
                    row = tile * 8 + half * 4
                    out_ref[(tile * 2 + half) * 4 + c] = acc[row : row + 4, c * 128 : (c + 1) * 128].astype(BF16)


def sum_kernel(in_ref, out_ref):
    for c in range(3):
        total = in_ref[c].astype(F32)
        for p in range(1, PARTS):
            total = total + in_ref[3 * p + c].astype(F32)
        total = total.astype(BF16)
        for p in range(PARTS):
            out_ref[3 * p + c] = total


def place_kernel(in_ref, self_ref, neigh_ref):
    for tile in range(12):
        for half in range(2):
            for c in range(4):
                value = in_ref[(tile * 2 + half) * 4 + c].astype(F32)
                row = (tile % 6) * 8 + half * 4
                ref = self_ref if tile < 6 else neigh_ref
                ref[row : row + 4, c * 128 : (c + 1) * 128] = value


def whole(shape):
    return pl.BlockSpec(shape, lambda *_: (0,) * len(shape))


def resident():
    return pl.BlockSpec(memory_space=pltpu.VMEM)


def near(x):
    return pltpu.with_memory_space_constraint(x, pltpu.VMEM)


def exchange(x, axis):
    return near(lax.all_to_all(x, axis, split_axis=0, concat_axis=0, tiled=True))


def body(features, neighbors, degree, send_rows, labels, w_self, w_neigh, bias, a_self, a_neigh):
    degree = degree.reshape(1, NP)
    labels = labels.reshape(1, NP)
    bias, a_self, a_neigh = bias.reshape(1, HID), a_self.reshape(1, HID), a_neigh.reshape(1, HID)

    outgoing = call(send_kernel, sds((SENT // 2, 128), BF16), "send")(features, send_rows)
    incoming = exchange(outgoing, "dom")

    steps = 1
    nbr_spec = pl.BlockSpec((FAN, NP // steps), lambda i: (0, i))
    deg_spec = pl.BlockSpec((1, NP // steps), lambda i: (0, i))
    col_spec = pl.BlockSpec((SL, NP // steps), lambda i: (0, i))
    own_spec = pl.BlockSpec((NB // steps, SL, 128), lambda i: (i, 0, 0))
    own = call(
        own_kernel,
        sds((NB, SL, 128), F32),
        "own",
        grid=(steps,),
        in_specs=[nbr_spec, deg_spec, whole((SL, NP))],
        out_specs=own_spec,
        scratch_shapes=[pltpu.VMEM((6 * OWN_FIELD, 128), BF16)] * 2 + [pltpu.VMEM((SL, NP), BF16)],
    )(neighbors, degree, features)
    block = call(
        finish_kernel,
        sds((NB, 2 * SL, 128), BF16),
        "finish",
        grid=(steps,),
        in_specs=[resident(), nbr_spec, deg_spec, own_spec, col_spec],
        out_specs=pl.BlockSpec((NB // steps, 2 * SL, 128), lambda i: (i, 0, 0)),
        scratch_shapes=[pltpu.VMEM((6 * FAR_FIELD, 128), BF16)] * 2 + [pltpu.VMEM((SL, SENT), BF16)],
    )(incoming, neighbors, degree, own, features)
    mine = exchange(block, "feat")

    mask, scores = call(preact_kernel, (sds((HID, 128), BF16), sds((NB, 8, 128), F32)), "preact")(
        mine, near(w_self), near(w_neigh), bias, a_self, a_neigh
    )
    scores = exchange(scores, "feat")
    masks = lax.all_gather(mask, "feat", axis=0, tiled=False)
    score_out = call(boundary_score_kernel, sds((PARTS, 1, 128), F32), "bscore")(scores, near(send_rows))
    score_in = exchange(score_out, "dom")

    logits, dlogit, slot, slot_out = call(
        logit_kernel,
        (sds((1, NP), F32), sds((1, NP), F32), sds((SLOTS // 128, 128), F32), sds((PARTS, 1, 128), F32)),
        "logit",
        scratch_shapes=[pltpu.VMEM((SLOTS // 128, 128), F32), pltpu.VMEM((3 * SLOTS // 128, 128), F32)],
    )(scores, score_in, neighbors, degree, labels)
    returned = exchange(slot_out, "dom")

    per = 4
    partial = call(
        grad_kernel,
        sds((96, 4, 128), BF16),
        "grad",
        grid=(NB // per,),
        in_specs=[
            resident(),
            whole((1, B, PARTS)),
            whole((SLOTS // 128, 128)),
            whole((1, NP)),
            whole((1, HID)),
            whole((1, HID)),
            pl.BlockSpec((per, HID, 128), lambda i: (i, 0, 0)),
            pl.BlockSpec((per, 2 * SL, 128), lambda i: (i, 0, 0)),
        ],
        out_specs=whole((96, 4, 128)),
        scratch_shapes=[
            pltpu.VMEM((1, NP), F32),
            pltpu.VMEM((HID, 128), F32),
            pltpu.VMEM((HID, 128), F32),
            pltpu.VMEM((2 * SL, HID), F32),
        ],
    )(returned, send_rows, slot, dlogit, a_self, a_neigh, masks, block)
    shares = exchange(partial, "dom")
    summed = call(sum_kernel, sds((96, 4, 128), BF16), "sum")(shares)
    summed = exchange(summed, "dom")
    grad_self, grad_neigh = call(place_kernel, (sds((SL, HID), F32), sds((SL, HID), F32)), "place")(summed)
    return (logits.reshape(NP), grad_self, grad_neigh)


def solution(mesh):
    return jax.shard_map(
        body,
        mesh=mesh,
        in_specs=(
            P("feat", "dom"),
            P(None, "dom"),
            P("dom"),
            P("dom", None, None),
            P("dom"),
            P(),
            P(),
            P(),
            P(),
            P(),
        ),
        out_specs=(P("dom"), P("feat", None), P("feat", None)),
        check_vma=False,
    )
```

```python
import jax
import jax.numpy as jnp
from jax import lax
from jax.experimental import pallas as pl
from jax.experimental.pallas import tpu as pltpu
from jax.sharding import PartitionSpec as P

F32 = jnp.float32
BF16 = jnp.bfloat16
I32 = jnp.int32

SL = 48
NP = 2048
NB = 16
PARTS = 32
B = 32
SENT = 1024
SLOTS = 3072
FAN = 16
HID = 512
OWN_FIELD = 352
FAR_FIELD = 176


def call(kernel, out_shape, name, **kw):
    return pl.pallas_call(kernel, out_shape=out_shape, name=name, **kw)


def sds(shape, dtype):
    return jax.ShapeDtypeStruct(shape, dtype)


def split3(x):
    hi = x.astype(BF16)
    rest = x - hi.astype(F32)
    mid = rest.astype(BF16)
    low = (rest - mid.astype(F32)).astype(BF16)
    return hi, mid, low


def send_kernel(feat_ref, send_ref, out_ref):
    feats = feat_ref[...]
    columns = jnp.transpose(send_ref[0], (1, 0))
    lanes = lax.broadcasted_iota(I32, (B, NP), 1)
    out_ref[...] = jnp.zeros_like(out_ref)
    for r in range(2):
        onehot = jnp.concatenate(
            [jnp.where(columns[:, p : p + 1] == lanes, 1.0, 0.0).astype(BF16) for p in range(4 * r, 4 * r + 4)], axis=0
        )
        rows = lax.dot_general(onehot, feats, (((1,), (1,)), ((), ())), preferred_element_type=F32).astype(BF16)
        for p in range(4):
            for h in range(2):
                taken = rows[32 * p + 16 * h : 32 * p + 16 * h + 16]
                out_ref[(4 * r + p) * 16 : (4 * r + p) * 16 + 16, 64 * h : 64 * h + SL] = taken


def build_counts(nbr_ref, deg_ref, cnt_ref, lanes, place, size, field, group):
    rows8 = lax.broadcasted_iota(I32, (8, 128), 0)
    idx = place(nbr_ref[:, lanes])
    valid = (lax.broadcasted_iota(I32, (FAN, 128), 0) < deg_ref[:, lanes]) & (idx >= 0) & (idx < size)
    which = jnp.zeros_like(idx)
    for j in range(1, 6):
        which = which + jnp.where(idx >= j * field, 1, 0)
    q = idx - which * field
    v = jnp.left_shift(jnp.ones_like(idx), which * 5)
    above = jnp.where(valid, lax.shift_right_arithmetic(q, group.bit_length() - 1), -1)
    below = jnp.bitwise_and(q, group - 1)
    aboves, tables = [], []
    for k in range(FAN):
        aboves.append(jnp.broadcast_to(above[k : k + 1], (8, 128)))
        low = jnp.broadcast_to(below[k : k + 1], (8, 128))
        value = jnp.broadcast_to(v[k : k + 1], (8, 128))
        tables.append([jnp.where(low == rows8 + 8 * c, value, 0) for c in range(group // 8)])
    for g in range(field // group):
        accs = [jnp.zeros((8, 128), I32)] * (group // 8)
        for k in range(FAN):
            hit = aboves[k] == g
            accs = [acc + jnp.where(hit, tables[k][c], 0) for c, acc in enumerate(accs)]
        for c in range(0, group // 8, 2):
            both = jnp.concatenate(accs[c : c + 2], axis=0)
            for j in range(6):
                count = jnp.bitwise_and(both, 31 << (5 * j)).astype(F32).astype(BF16)
                row = j * field + g * group + 8 * c
                cnt_ref[row : row + 16, :] = count


def scaled(values, field):
    slot = lax.broadcasted_iota(I32, values.shape, 1)
    scale = jnp.full(values.shape, 2.0**12, F32)
    for j in range(1, 6):
        scale = jnp.where(slot >= j * field, 2.0 ** (12 - 5 * j), scale)
    return (values.astype(F32) * scale).astype(BF16)


def pipelined(nbr_ref, deg_ref, buffers, place, size, field, group, multiply):
    def lanes(n):
        return pl.ds(pl.multiple_of(n * 128, 128), 128)

    def pair(n, carry):
        multiply(jnp.maximum(2 * n - 1, 0), buffers[1])
        build_counts(nbr_ref, deg_ref, buffers[0], lanes(2 * n), place, size, field, group)
        multiply(2 * n, buffers[0])
        build_counts(nbr_ref, deg_ref, buffers[1], lanes(2 * n + 1), place, size, field, group)
        return carry

    blocks = deg_ref.shape[1] // 128
    lax.fori_loop(0, blocks // 2, pair, 0)
    multiply(blocks - 1, buffers[1])


def own_kernel(nbr_ref, deg_ref, feat_ref, own_ref, cnt0, cnt1, feats):
    @pl.when(pl.program_id(0) == 0)
    def _():
        feats[...] = scaled(feat_ref[...], OWN_FIELD)

    def multiply(n, cnt):
        own_ref[n] = jnp.dot(feats[...], cnt[0:NP, :], preferred_element_type=F32)

    pipelined(nbr_ref, deg_ref, (cnt0, cnt1), lambda idx: idx, NP, OWN_FIELD, 32, multiply)


def finish_kernel(recv_ref, nbr_ref, deg_ref, own_ref, feat_ref, out_ref, cnt0, cnt1, recv):
    @pl.when(pl.program_id(0) == 0)
    def _():
        both = jnp.transpose(recv_ref[...].astype(F32), (1, 0))
        recv[...] = scaled(jnp.concatenate([both[0:SL], both[64 : 64 + SL]], axis=1), FAR_FIELD)

    def place(idx):
        far = idx - NP
        part = jnp.bitwise_and(lax.shift_right_arithmetic(far, 4), 1)
        row = lax.shift_right_arithmetic(far, 5) * 16 + jnp.bitwise_and(far, 15)
        return jnp.where(far < 0, -1, part * (SENT // 2) + row)

    def multiply(n, cnt):
        lanes = pl.ds(pl.multiple_of(n * 128, 128), 128)
        far = jnp.dot(recv[...], cnt[0:SENT, :], preferred_element_type=F32)
        inverse = 1.0 / deg_ref[:, lanes].astype(F32)
        out_ref[n, 0:SL, :] = feat_ref[:, lanes]
        out_ref[n, SL : 2 * SL, :] = ((own_ref[n] + far) * 2.0**-12 * inverse).astype(BF16)

    pipelined(nbr_ref, deg_ref, (cnt0, cnt1), place, SENT, FAR_FIELD, 16, multiply)


def columns(*refs):
    rows = [ref[...] for ref in refs] + [jnp.zeros((8 - len(refs), HID), F32)]
    return jnp.transpose(jnp.concatenate(rows, axis=0), (1, 0))


def preact_kernel(block_ref, ws_ref, wn_ref, bias_ref, as_ref, an_ref, mask_ref, score_ref):
    dims = (((0,), (0,)), ((), ()))
    pre = lax.dot_general(block_ref[:, 0:SL, :].reshape(SL * NB, 128), ws_ref[...], dims, preferred_element_type=F32)
    pre = pre + lax.dot_general(block_ref[:, SL : 2 * SL, :].reshape(SL * NB, 128), wn_ref[...], dims, preferred_element_type=F32)
    par = columns(bias_ref, as_ref, an_ref)
    pre = jnp.transpose(pre, (1, 0)) + par[:, 0:1]
    hidden = jnp.maximum(pre, 0.0)
    mask_ref[...] = jnp.where(pre > 0, 1.0, 0.0).astype(BF16)
    own = jnp.sum(hidden * par[:, 1:2], axis=0, keepdims=True)
    neigh = jnp.sum(hidden * par[:, 2:3], axis=0, keepdims=True)
    both = jnp.concatenate([own, neigh], axis=0)
    for b in range(NB):
        score_ref[b] = both


def lane_gather(row, idx):
    return jnp.take_along_axis(jnp.broadcast_to(row, idx.shape), idx, axis=1)


def boundary_score_kernel(score_ref, send_ref, out_ref):
    idx = jnp.concatenate([send_ref[0], jnp.zeros((PARTS, 96), I32)], axis=1)
    low = jnp.bitwise_and(idx, 127)
    high = lax.shift_right_logical(idx, 7)
    acc = jnp.zeros((PARTS, 128), F32)
    for b in range(NB):
        acc = jnp.where(high == b, lane_gather(score_ref[b, 1:2, :], low), acc)
    for p in range(PARTS):
        out_ref[p] = acc[p : p + 1, :]


def dense_rows(parts, dtype=F32):
    lane = lax.broadcasted_iota(I32, (8, 128), 1)
    acc = jnp.zeros((8, 128), dtype)
    for g in range(4):
        rows = jnp.concatenate([parts[4 * r + g] for r in range(8)], axis=0)
        rows = pltpu.roll(rows, 32 * g, 1) if g else rows
        acc = jnp.where(lax.shift_right_logical(lane, 5) == g, rows, acc)
    return acc


def logit_kernel(score_ref, far_ref, nbr_ref, deg_ref, label_ref, logit_ref, dlogit_ref, slot_ref, out_ref, table, acc_ref):
    for b in range(NB):
        table[b : b + 1, :] = score_ref[b, 1:2, :]
    table[NB:, :] = dense_rows(far_ref)
    acc_ref[...] = jnp.zeros_like(acc_ref)
    highs = SLOTS // 128
    high_rows = lax.broadcasted_iota(I32, (highs, 128), 0)
    low_rows = lax.broadcasted_iota(I32, (16, 128), 0)
    one16, zero16 = jnp.ones((16, 128), BF16), jnp.zeros((16, 128), BF16)

    def one(f, left, right):
        lanes = pl.ds(pl.multiple_of(f * 128, 128), 128)
        idx = nbr_ref[:, lanes]
        low = jnp.bitwise_and(idx, 127)
        high = lax.shift_right_logical(idx, 7)
        acc = jnp.zeros((FAN, 128), F32)
        for r in range(SLOTS // 128):
            acc = jnp.where(high == r, lane_gather(table[r : r + 1, :], low), acc)
        degree = deg_ref[:, lanes]
        valid = lax.broadcasted_iota(I32, (FAN, 128), 0) < degree
        inverse = 1.0 / degree.astype(F32)
        total = jnp.sum(jnp.where(valid, acc, 0.0), axis=0, keepdims=True)
        logits = score_ref[f, 0:1, :] + total * inverse
        logit_ref[:, lanes] = logits
        dlogit = (jax.nn.sigmoid(logits) - label_ref[:, lanes].astype(F32)) * (float(NP * PARTS) ** -0.5)
        dlogit_ref[:, lanes] = dlogit
        thirds = [t.astype(F32) for t in split3(dlogit * inverse)]
        high = jnp.where(valid, high, -1)
        for k in range(FAN):
            hit = high[k : k + 1] == high_rows
            left.append(jnp.concatenate([jnp.where(hit, t, 0.0) for t in thirds], axis=0).astype(BF16))
            offset = (jnp.broadcast_to(low[k : k + 1], (16, 128)) - low_rows).astype(F32).astype(BF16)
            right.append(jnp.concatenate([jnp.where(offset == 16.0 * j, one16, zero16) for j in range(8)], axis=0))

    def several(n, carry):
        left, right = [], []
        for u in range(4):
            one(4 * n + u, left, right)
        acc_ref[...] += lax.dot_general(
            jnp.concatenate(left, axis=1),
            jnp.concatenate(right, axis=1),
            (((1,), (1,)), ((), ())),
            preferred_element_type=F32,
        )
        return carry

    lax.fori_loop(0, NB // 4, several, 0)
    slot = acc_ref[0:highs] + acc_ref[highs : 2 * highs] + acc_ref[2 * highs : 3 * highs]
    slot_ref[...] = slot
    for r in range(8):
        row = slot[NB + r : NB + r + 1, :]
        for g in range(4):
            out_ref[4 * r + g] = pltpu.roll(row, 128 - 32 * g, 1) if g else row


def grad_kernel(ret_ref, send_ref, slot_ref, dlogit_ref, as_ref, an_ref, mask_ref, block_ref, out_ref, dneigh, wide_s, wide_n, acc):
    step = pl.program_id(0)
    per = mask_ref.shape[0]

    @pl.when(step == 0)
    def _():
        send = jnp.concatenate([send_ref[0], jnp.zeros((PARTS, 96), I32)], axis=1)
        send = dense_rows([send[p : p + 1] for p in range(PARTS)], I32)
        thirds = [t.astype(F32) for t in split3(dense_rows(ret_ref))]
        low = jnp.bitwise_and(send, 127)
        high = lax.shift_right_logical(send, 7)
        high_rows = lax.broadcasted_iota(I32, (NB, 128), 0)
        low_rows = lax.broadcasted_iota(I32, (128, 128), 0)
        left, right = [], []
        for r in range(SENT // 128):
            hit = high[r : r + 1] == high_rows
            left.append(jnp.concatenate([jnp.where(hit, t[r : r + 1], 0.0) for t in thirds], axis=0).astype(BF16))
            right.append(jnp.where(low[r : r + 1] == low_rows, 1.0, 0.0).astype(BF16))
        sums = lax.dot_general(
            jnp.concatenate(left, axis=1),
            jnp.concatenate(right, axis=1),
            (((1,), (1,)), ((), ())),
            preferred_element_type=F32,
        )
        sums = slot_ref[0:NB] + (sums[0:NB] + sums[NB : 2 * NB] + sums[2 * NB : 3 * NB])
        for f in range(NB):
            dneigh[:, f * 128 : (f + 1) * 128] = sums[f : f + 1]
        par = columns(as_ref, an_ref)
        wide_s[...] = jnp.broadcast_to(par[:, 0:1], (HID, 128))
        wide_n[...] = jnp.broadcast_to(par[:, 1:2], (HID, 128))
        acc[...] = jnp.zeros_like(acc)

    for b in range(per):
        lanes = pl.ds(pl.multiple_of((step * per + b) * 128, 128), 128)
        grad = wide_s[...] * dlogit_ref[:, lanes] + wide_n[...] * dneigh[:, lanes]
        dpre = grad.astype(BF16) * mask_ref[b]
        acc[...] += lax.dot_general(block_ref[b], dpre, (((1,), (1,)), ((), ())), preferred_element_type=F32)

    @pl.when(step == pl.num_programs(0) - 1)
    def _():
        for tile in range(12):
            for half in range(2):
                for c in range(4):
                    row = tile * 8 + half * 4
                    out_ref[(tile * 2 + half) * 4 + c] = acc[row : row + 4, c * 128 : (c + 1) * 128].astype(BF16)


def sum_kernel(in_ref, out_ref):
    for c in range(3):
        total = in_ref[c].astype(F32)
        for p in range(1, PARTS):
            total = total + in_ref[3 * p + c].astype(F32)
        total = total.astype(BF16)
        for p in range(PARTS):
            out_ref[3 * p + c] = total


def place_kernel(in_ref, self_ref, neigh_ref):
    for tile in range(12):
        for half in range(2):
            for c in range(4):
                value = in_ref[(tile * 2 + half) * 4 + c].astype(F32)
                row = (tile % 6) * 8 + half * 4
                ref = self_ref if tile < 6 else neigh_ref
                ref[row : row + 4, c * 128 : (c + 1) * 128] = value


def whole(shape):
    return pl.BlockSpec(shape, lambda *_: (0,) * len(shape))


def resident():
    return pl.BlockSpec(memory_space=pltpu.VMEM)


def near(x):
    return pltpu.with_memory_space_constraint(x, pltpu.VMEM)


def exchange(x, axis):
    return near(lax.all_to_all(x, axis, split_axis=0, concat_axis=0, tiled=True))


def body(features, neighbors, degree, send_rows, labels, w_self, w_neigh, bias, a_self, a_neigh):
    degree = degree.reshape(1, NP)
    labels = labels.reshape(1, NP)
    bias, a_self, a_neigh = bias.reshape(1, HID), a_self.reshape(1, HID), a_neigh.reshape(1, HID)

    outgoing = call(
        send_kernel,
        sds((SENT // 2, 128), BF16),
        "send",
        grid=(4,),
        in_specs=[whole((SL, NP)), pl.BlockSpec((1, PARTS // 4, B), lambda i: (0, i, 0))],
        out_specs=pl.BlockSpec((SENT // 8, 128), lambda i: (i, 0)),
    )(features, send_rows)
    incoming = exchange(outgoing, "dom")

    steps = 1
    nbr_spec = pl.BlockSpec((FAN, NP // steps), lambda i: (0, i))
    deg_spec = pl.BlockSpec((1, NP // steps), lambda i: (0, i))
    col_spec = pl.BlockSpec((SL, NP // steps), lambda i: (0, i))
    own_spec = pl.BlockSpec((NB // steps, SL, 128), lambda i: (i, 0, 0))
    own = call(
        own_kernel,
        sds((NB, SL, 128), F32),
        "own",
        grid=(steps,),
        in_specs=[nbr_spec, deg_spec, whole((SL, NP))],
        out_specs=own_spec,
        scratch_shapes=[pltpu.VMEM((6 * OWN_FIELD, 128), BF16)] * 2 + [pltpu.VMEM((SL, NP), BF16)],
    )(neighbors, degree, features)
    block = call(
        finish_kernel,
        sds((NB, 2 * SL, 128), BF16),
        "finish",
        grid=(steps,),
        in_specs=[resident(), nbr_spec, deg_spec, own_spec, col_spec],
        out_specs=pl.BlockSpec((NB // steps, 2 * SL, 128), lambda i: (i, 0, 0)),
        scratch_shapes=[pltpu.VMEM((6 * FAR_FIELD, 128), BF16)] * 2 + [pltpu.VMEM((SL, SENT), BF16)],
    )(incoming, neighbors, degree, own, features)
    mine = exchange(block, "feat")

    mask, scores = call(preact_kernel, (sds((HID, 128), BF16), sds((NB, 2, 128), F32)), "preact")(
        mine, near(w_self), near(w_neigh), bias, a_self, a_neigh
    )
    scores = exchange(scores, "feat")
    masks = lax.all_gather(mask, "feat", axis=0, tiled=False)
    score_out = call(boundary_score_kernel, sds((PARTS, 1, 128), F32), "bscore")(scores, near(send_rows))
    score_in = exchange(score_out, "dom")

    logits, dlogit, slot, slot_out = call(
        logit_kernel,
        (sds((1, NP), F32), sds((1, NP), F32), sds((SLOTS // 128, 128), F32), sds((PARTS, 1, 128), F32)),
        "logit",
        scratch_shapes=[pltpu.VMEM((SLOTS // 128, 128), F32), pltpu.VMEM((3 * SLOTS // 128, 128), F32)],
    )(scores, score_in, neighbors, degree, labels)
    returned = exchange(slot_out, "dom")

    per = 4
    partial = call(
        grad_kernel,
        sds((96, 4, 128), BF16),
        "grad",
        grid=(NB // per,),
        in_specs=[
            resident(),
            whole((1, B, PARTS)),
            whole((SLOTS // 128, 128)),
            whole((1, NP)),
            whole((1, HID)),
            whole((1, HID)),
            pl.BlockSpec((per, HID, 128), lambda i: (i, 0, 0)),
            pl.BlockSpec((per, 2 * SL, 128), lambda i: (i, 0, 0)),
        ],
        out_specs=whole((96, 4, 128)),
        scratch_shapes=[
            pltpu.VMEM((1, NP), F32),
            pltpu.VMEM((HID, 128), F32),
            pltpu.VMEM((HID, 128), F32),
            pltpu.VMEM((2 * SL, HID), F32),
        ],
    )(returned, send_rows, slot, dlogit, a_self, a_neigh, masks, block)
    shares = exchange(partial, "dom")
    summed = call(sum_kernel, sds((96, 4, 128), BF16), "sum")(shares)
    summed = exchange(summed, "dom")
    grad_self, grad_neigh = call(place_kernel, (sds((SL, HID), F32), sds((SL, HID), F32)), "place")(summed)
    return (logits.reshape(NP), grad_self, grad_neigh)


def solution(mesh):
    return jax.shard_map(
        body,
        mesh=mesh,
        in_specs=(
            P("feat", "dom"),
            P(None, "dom"),
            P("dom"),
            P("dom", None, None),
            P("dom"),
            P(),
            P(),
            P(),
            P(),
            P(),
        ),
        out_specs=(P("dom"), P("feat", None), P("feat", None)),
        check_vma=False,
    )
```
